256 devices in a mesh: head: 4 (over z_lo, core), seq: 4 (over x), req: 16 (over z_hi, y).
Axes of the slice: x: 4, y: 4, z: 8 (z_hi: 4, z_lo: 2; z = z_hi * 2 + z_lo), core: 2. Of those that a mesh axis runs over, the one named last changes fastest.
Arguments:
- stream: bfloat16 [8192, 2048], P(('req', 'seq', 'head')), may hold values from -12 to 12
- queries: bfloat16 [8192, 4096], P(('req', 'seq'), 'head'), may hold values from -16 to 16
- cache_pairs: bfloat16 [8192, 4, 128, 256], P(('req', 'seq'), 'head'), may hold values from -16 to 16
- fresh_pairs: bfloat16 [8192, 4, 256], P(('req', 'seq'), 'head'), may hold values from -16 to 16
- kept_slots: int32 [8192, 4, 96], P(('req', 'seq'), 'head'), may hold values from 0 to 31, as said below
- segment_kept_count: int32 [8192, 4, 4], P(('req', 'seq'), 'head'), may hold values from 1 to 24, 60 in all within a row
- output_weight: bfloat16 [4096, 2048], P('head', 'seq'), may hold values from -0.09375 to 0.09375
- norm_gain: float32 [2048], replicated, may hold values from 0.1 to 1.9
- routes: int32 [8192, 8], P(('req', 'seq', 'head')), may hold values from 0 to 63, all different within a row; in each aligned block of 32 rows (0 to 31, 32 to 63, ...) at most 8 rows name the same one
- gate_codes: int32 [8192, 8], P(('req', 'seq', 'head')), may hold values from 1 to 16
- gate_weight: bfloat16 [64, 2048, 768], P(('seq', 'req')), may hold values from -0.125 to 0.125
- up_weight: bfloat16 [64, 2048, 768], P(('seq', 'req')), may hold values from -0.125 to 0.125
- down_weight: bfloat16 [64, 768, 2048], P(('seq', 'req')), may hold values from -0.21875 to 0.21875
Outputs:
- layer_out: bfloat16 [8192, 2048], P(('req', 'seq', 'head'))
The draws below stay inside these ranges and needn't reach their ends.
Inputs may be any that keep to these rules, and one draw needn't show every extreme that they name: `kept_slots`: entries s * 24 to (s + 1) * 24 - 1 of a list are distinct positions within segment s, counted from the segment's start; only the first segment_kept_count[r, h, s] of them are used. `segment_kept_count`: the 4 counts of a request's head add up to 60. `routes`: A token names 8 different experts. In each aligned block of 32 rows (the tokens of one device) no expert is named more than 8 times.
All inputs are finite; a program needn't handle non-finite values.
Results may differ from the reference program's by a relative error of at most 0.01.
Values may be sent and summed in bfloat16 or wider, within the bound.
No kernel may reach another device: no remote copies, remote signals or barrier semaphores. Data moves between devices by JAX's collectives and lax.ppermute only.
A program may use at most 128 MiB of HBM per device.

```python
import math
import jax
import jax.numpy as jnp
import numpy as np
from jax import lax

D = 2048
QUERY_HEADS = 32
KEY_VALUE_HEADS = 4
HEAD_WIDTH = 128
FF = 768
TOPK = 8
TOK_DEV = 32
CACHE_SEGMENTS = 4
SEGMENT_LENGTH = 32
SEGMENT_KEPT_MAX = 24
REQUEST_COUNT = 8192
CONTEXT_LENGTH = 128
KEPT_PER_HEAD = 60
E = 64
CAP = 8


def draw_stream(key, part):
    values = jax.random.normal(jax.random.fold_in(key, 11), (REQUEST_COUNT, D), jnp.float32)
    return jnp.clip(values, -12.0, 12.0).astype(jnp.bfloat16)


def draw_queries(key, part):
    query_shape = (REQUEST_COUNT, QUERY_HEADS * HEAD_WIDTH)
    values = 2.0 * jax.random.normal(jax.random.fold_in(key, 21), query_shape, jnp.float32)
    return jnp.clip(values, -16.0, 16.0).astype(jnp.bfloat16)


def raised_index_pairs(key, salt, pair_shape):
    values = jax.random.normal(jax.random.fold_in(key, salt), pair_shape, jnp.float32)
    return jnp.clip(values, -16.0, 16.0).astype(jnp.bfloat16)


def draw_cache_pairs(key, part):
    return raised_index_pairs(key, 31, (REQUEST_COUNT, KEY_VALUE_HEADS, CONTEXT_LENGTH, 2 * HEAD_WIDTH))


def draw_fresh_pairs(key, part):
    return raised_index_pairs(key, 41, (REQUEST_COUNT, KEY_VALUE_HEADS, 2 * HEAD_WIDTH))


def draw_kept_slots(key, part):
    unscaled_scores = jax.random.randint(jax.random.fold_in(key, 51), (REQUEST_COUNT, KEY_VALUE_HEADS, CACHE_SEGMENTS, SEGMENT_LENGTH), 0, 1 << 19)
    distinct = unscaled_scores * SEGMENT_LENGTH + jnp.arange(SEGMENT_LENGTH, dtype=jnp.int32)
    sorted_order = jnp.argsort(distinct, axis=-1)
    return sorted_order[..., :SEGMENT_KEPT_MAX].reshape(REQUEST_COUNT, KEY_VALUE_HEADS, CACHE_SEGMENTS * SEGMENT_KEPT_MAX).astype(jnp.int32)


def place_ends(entries, stream_key, low, high):
    dims = entries.shape
    place = [jax.random.randint(jax.random.fold_in(stream_key, axis), (), 0, dims[axis]) for axis in range(len(dims))]
    entries = entries.at[tuple(place)].set(low)
    longest = dims.index(max(dims))
    place[longest] = (place[longest] + 1) % dims[longest]
    return entries.at[tuple(place)].set(high)


def levels(rng, dims, cuts, low, high):
    gain, own = 1.0, jax.random.fold_in(rng, 6)
    for dim, parts in cuts:
        steps = jnp.exp(jax.random.uniform(jax.random.fold_in(own, dim), (parts,), jnp.float32, low / len(cuts), high / len(cuts)))
        gain = gain * jnp.repeat(steps, dims[dim] // parts).reshape([-1 if axis == dim else 1 for axis in range(len(dims))])
    return gain


def length_profile(number_of, total, bound, skew):
    portions = [(1 << 20) // math.isqrt(standing ** skew) + 1 for standing in range(2, number_of + 1)]
    rest, counts = total - bound - (number_of - 1), [1] * (number_of - 1)
    while rest > 0:
        free = [i for i in range(number_of - 1) if counts[i] < bound]
        pool, remaining = sum([portions[i] for i in free]), rest
        for i in free:
            extra = min(bound - counts[i], max(1, remaining * portions[i] // pool), rest)
            counts[i] = counts[i] + extra
            rest = rest - extra
    return np.array([bound] + counts)


def uneven(stream_key, count, total, most, lean):
    if count == 2:
        one = jax.random.randint(stream_key, (), max(1, total - most), min(most, total - 1) + 1)
        return jnp.stack([one, total - one])
    tallies = jnp.asarray(length_profile(count, total, most, lean), jnp.int32)
    couples = (count - 1) // 2
    source_of, taker = tallies[1:1 + 2 * couples:2], tallies[2:2 + 2 * couples:2]
    margin = jnp.minimum(source_of - 1, most - taker)
    shifted = jax.random.randint(jax.random.fold_in(stream_key, 1), (couples,), 0, 1 << 20) % (margin + 1)
    tallies = tallies.at[1:1 + 2 * couples:2].set(source_of - shifted).at[2:2 + 2 * couples:2].set(taker + shifted)
    return tallies[jax.random.permutation(jax.random.fold_in(stream_key, 2), count)]


def deal_out(key, own, number, rows, amount, top, bound, skew):
    order = jax.random.permutation(key, amount)
    heavy_load, common = load_shares(amount, rows * top, bound, skew, True), load_shares(amount, rows * top, bound, skew, False)
    places = jnp.arange(amount)

    def named(tallies, rotation):
        used = int((tallies > 0).sum())
        fixed = max(1, used // 4)
        moved = fixed + (places - fixed + rotation * (used - fixed)) % max(1, amount - fixed)
        return jnp.zeros((amount,), jnp.int32).at[order[jnp.where(places < fixed, places, moved)]].set(jnp.asarray(tallies, jnp.int32))

    tallies = jnp.where(number % 4 == 0, named(heavy_load, number // 4), named(common, number - number // 4 - 1))
    mixed = jax.random.permutation(jax.random.fold_in(own, 3), amount)
    donor, taker = mixed[0:amount // 2 * 2:2], mixed[1:amount // 2 * 2:2]
    margin = jnp.minimum(tallies[donor] - 1, bound - tallies[taker]) // 2
    margin = jnp.where((donor == order[0]) | (taker == order[0]) | (tallies[taker] == 0), 0, jnp.maximum(margin, 0))
    moved = jax.random.randint(jax.random.fold_in(own, 4), (amount // 2,), 0, 1 << 20) % (margin + 1)
    tallies = tallies.at[donor].add(-moved).at[taker].add(moved)
    labels = jnp.searchsorted(jnp.cumsum(tallies), jnp.arange(rows * top), side="right").astype(jnp.int32)
    table = labels.reshape(top, rows).T
    table = table[jax.random.permutation(jax.random.fold_in(own, 1), rows)]
    rotation = jax.random.randint(jax.random.fold_in(own, 2), (rows, 1), 0, top)
    return jnp.take_along_axis(table, (jnp.arange(top)[None, :] + rotation) % top, axis=1)


def load_shares(number_of, total, reach, slope, full):
    portions = [(1 << 20) // math.isqrt(rank ** slope) + 1 for rank in range(1, number_of + 1)]
    largest = reach if full else min(reach, max(-(-total // number_of), total * portions[0] // sum(portions)))
    least = 1 if total - largest >= number_of - 1 else 0
    given, spare = [largest] + [least] * (number_of - 1), total - largest - least * (number_of - 1)
    while spare > 0:
        candidates = [i for i in range(1, number_of) if given[i] < largest] or [i for i in range(1, number_of) if given[i] < reach]
        whole, remaining = sum([portions[i] for i in candidates]), spare
        for i in candidates:
            extra = min(reach - given[i], max(1, remaining * portions[i] // whole), spare)
            given[i] = given[i] + extra
            spare = spare - extra
    return np.array(given)


def bell_draw(own_key, shape, scale, most, cuts=(), kind=jnp.bfloat16):
    gain = levels(own_key, shape, cuts, -0.22, 0.18) if cuts else 1.0
    entries = jax.random.normal(own_key, shape, jnp.float32) * scale * gain
    return jnp.minimum(jnp.maximum(entries, -most), most).astype(kind)


def setup_inputs(seed: int = 0) -> dict:
    splits = jax.random.split(jax.random.key(seed), 14)
    stream = draw_stream(jax.random.fold_in(splits[13], 71), 0)
    queries = draw_queries(jax.random.fold_in(splits[13], 71), 0)
    cache_pairs = draw_cache_pairs(jax.random.fold_in(splits[13], 71), 0)
    fresh_pairs = draw_fresh_pairs(jax.random.fold_in(splits[13], 71), 0)
    kept_slots = draw_kept_slots(jax.random.fold_in(splits[13], 71), 0)
    segment_kept_count = jax.vmap(lambda own: uneven(own, CACHE_SEGMENTS, KEPT_PER_HEAD, SEGMENT_KEPT_MAX, 2))(jax.random.split(splits[5], REQUEST_COUNT * KEY_VALUE_HEADS)).reshape((REQUEST_COUNT, KEY_VALUE_HEADS, CACHE_SEGMENTS)).astype(jnp.int32)
    output_weight = bell_draw(splits[6], (QUERY_HEADS * HEAD_WIDTH, D), (QUERY_HEADS * HEAD_WIDTH) ** -0.5, 0.09375, ((0, 4), (1, 4)))
    norm_gain = jnp.clip(1.0 + 0.18 * jax.random.normal(splits[7], (D,), jnp.float32), 0.1, 1.9)
    routes_keys = jax.random.split(jax.random.fold_in(splits[8], 1), REQUEST_COUNT // TOK_DEV)
    routes_turns = jax.random.permutation(jax.random.fold_in(splits[8], 3), REQUEST_COUNT // TOK_DEV)
    routes = jax.vmap(lambda own, number: deal_out(jax.random.fold_in(splits[8], 2), own, number, TOK_DEV, E, TOPK, CAP, 2))(routes_keys, routes_turns).reshape((REQUEST_COUNT, TOPK))
    gate_codes = place_ends(jax.random.randint(splits[9], (REQUEST_COUNT, TOPK), 1, 17), jax.random.fold_in(splits[9], 1), 1, 16).astype(jnp.int32)
    gate_weight = bell_draw(splits[10], (E, D, FF), D ** -0.5, 0.125, ((0, 64),))
    up_weight = bell_draw(splits[11], (E, D, FF), D ** -0.5, 0.125, ((0, 64),))
    down_weight = bell_draw(splits[12], (E, FF, D), FF ** -0.5, 0.21875, ((0, 64),))
    return {"stream": stream, "queries": queries, "cache_pairs": cache_pairs, "fresh_pairs": fresh_pairs, "kept_slots": kept_slots, "segment_kept_count": segment_kept_count, "output_weight": output_weight, "norm_gain": norm_gain, "routes": routes, "gate_codes": gate_codes, "gate_weight": gate_weight, "up_weight": up_weight, "down_weight": down_weight}


def attend_one(single_query_row, cache_entry_row, kept_slot_row, count_row, fresh_row):
    query_group_width = QUERY_HEADS // KEY_VALUE_HEADS
    query_matrix = single_query_row.reshape(KEY_VALUE_HEADS, query_group_width, HEAD_WIDTH).astype(jnp.float32)
    segment_starts = (jnp.arange(CACHE_SEGMENTS, dtype=jnp.int32) * SEGMENT_LENGTH)[None, :, None]
    cache_location = (kept_slot_row.reshape(KEY_VALUE_HEADS, CACHE_SEGMENTS, SEGMENT_KEPT_MAX) + segment_starts).astype(jnp.int32)
    selected_entries = jnp.take_along_axis(cache_entry_row, cache_location.reshape(KEY_VALUE_HEADS, CACHE_SEGMENTS * SEGMENT_KEPT_MAX)[:, :, None], axis=1)
    selected_entries = selected_entries.reshape(KEY_VALUE_HEADS, CACHE_SEGMENTS, SEGMENT_KEPT_MAX, 2 * HEAD_WIDTH).astype(jnp.float32)
    key_part = selected_entries[..., :HEAD_WIDTH]
    value_part = selected_entries[..., HEAD_WIDTH:]
    score_scale = HEAD_WIDTH ** (-0.5)
    scores = jnp.einsum('hgd,hskd->hsgk', query_matrix, key_part) * score_scale
    valid_mask = jnp.arange(SEGMENT_KEPT_MAX, dtype=jnp.int32)[None, None, None, :] < count_row[:, :, None, None]
    seg_max = lax.optimization_barrier(jnp.max(jnp.where(valid_mask, scores, -jnp.inf), axis=-1))
    rounded = jnp.where(valid_mask, jnp.exp(scores - seg_max[..., None]), 0.0).astype(jnp.bfloat16)
    soft_probs = lax.optimization_barrier(rounded).astype(jnp.float32)
    seg_sum = lax.optimization_barrier(jnp.sum(soft_probs, axis=-1))
    seg_acc = jnp.einsum('hsgk,hskd->hsgd', soft_probs, value_part)
    top_score = lax.optimization_barrier(jnp.max(seg_max, axis=1))
    factor = jnp.exp(seg_max - top_score[:, None, :])
    denom_sum = lax.optimization_barrier(jnp.sum(factor * seg_sum, axis=1))
    numer_sum = lax.optimization_barrier(jnp.sum(factor[..., None] * seg_acc, axis=1))
    fresh_float = fresh_row.astype(jnp.float32)
    own_score = jnp.einsum('hgd,hd->hg', query_matrix, fresh_float[:, :HEAD_WIDTH]) * score_scale
    new_top = jnp.maximum(top_score, own_score)
    keep_old = jnp.exp(top_score - new_top)
    take_new = jnp.exp(own_score - new_top)
    denom_sum = denom_sum * keep_old + take_new
    numer_sum = numer_sum * keep_old[..., None] + take_new[..., None] * fresh_float[:, None, HEAD_WIDTH:]
    return (numer_sum / denom_sum[..., None]).reshape(QUERY_HEADS * HEAD_WIDTH).astype(jnp.bfloat16)

def reference(stream, queries, cache_pairs, fresh_pairs, kept_slots, segment_kept_count, output_weight, norm_gain, routes, gate_codes, gate_weight, up_weight, down_weight):
    head_out = lax.map(lambda packed: attend_one(*packed), (queries, cache_pairs, kept_slots, segment_kept_count, fresh_pairs))
    attention = jnp.dot(head_out, output_weight, preferred_element_type=jnp.float32)
    residual = (stream.astype(jnp.float32) + attention).astype(jnp.bfloat16)
    widened = residual.astype(jnp.float32)
    normed = (widened * lax.rsqrt(lax.optimization_barrier(jnp.mean(widened * widened, axis=-1, keepdims=True)) + 1e-06) * norm_gain).astype(jnp.bfloat16)
    code_float = gate_codes.astype(jnp.float32)
    weights = code_float / lax.optimization_barrier(jnp.sum(code_float, axis=-1, keepdims=True))
    row_limit = min(REQUEST_COUNT, CAP * (REQUEST_COUNT // TOK_DEV))
    order_score = (REQUEST_COUNT - jnp.arange(REQUEST_COUNT, dtype=jnp.int32)).astype(jnp.int32)

    def expert_step(mixture, packed):
        gate_mat, up_mat, down_mat, expert = packed
        hit_mask = routes == expert
        share_of = lax.optimization_barrier(jnp.sum(jnp.where(hit_mask, weights, 0.0), axis=-1))
        present = jnp.any(hit_mask, axis=-1)
        unused, chosen = lax.top_k(jnp.where(present, order_score, 0).astype(jnp.int32), row_limit)
        selected_entries = normed[chosen]
        gate_val = jnp.dot(selected_entries, gate_mat, preferred_element_type=jnp.float32)
        upward = jnp.dot(selected_entries, up_mat, preferred_element_type=jnp.float32)
        activated = (jax.nn.silu(gate_val) * upward).astype(jnp.bfloat16)
        result = jnp.dot(activated, down_mat, preferred_element_type=jnp.float32)
        mixture = mixture.at[chosen].add(share_of[chosen][:, None] * result)
        return (mixture, None)
    mixture, unused = lax.scan(expert_step, jnp.zeros((REQUEST_COUNT, D), jnp.float32), (gate_weight, up_weight, down_weight, jnp.arange(E, dtype=jnp.int32)))
    return (residual.astype(jnp.float32) + mixture).astype(jnp.bfloat16)
```

```python
import jax
import jax.numpy as jnp
from jax import lax
from jax.experimental import pallas as pl
from jax.experimental.pallas import tpu as pltpu
from jax.sharding import Mesh
from jax.sharding import PartitionSpec as P

epsilon = 1e-06
LANES = 128
ATT_BLOCK = 32
HID_BLOCK = 256
MESH_AXES = ("zl", "core", "seq", "zh", "y")
PLANE = ("seq", "y")
HEADS = ("zl", "core")
STEPS = (0, 1, 3, 2)


def iota(shape, dim):
    return lax.broadcasted_iota(jnp.int32, shape, dim)


def div(a, b):
    return lax.div(a, jnp.full_like(a, b))


def rem(a, b):
    return lax.rem(a, jnp.full_like(a, b))


def attention_body(slots_ref, counts_ref, query_ref, cache_ref, fresh_ref, out_ref, bias_ref):
    rows, _, positions, pair = cache_ref.shape
    head_dim = pair // 2
    group = query_ref.shape[1] // head_dim
    scale = head_dim ** (-0.5)
    step = pl.program_id(0)

    @pl.when(step == 0)
    def _():
        listed, all_rows = slots_ref.shape
        segments = counts_ref.shape[0]
        keep = listed // segments
        seg_length = positions // segments
        counts = counts_ref[...].astype(jnp.float32)
        limit = jnp.concatenate(
            [jnp.broadcast_to(counts[s : s + 1], (keep, all_rows)) for s in range(segments)], axis=0
        )
        rank = rem(iota((listed, all_rows), 0), keep).astype(jnp.float32)
        valid = jnp.where(rank < limit, slots_ref[...].astype(jnp.float32), 99.0)
        valid = valid.astype(jnp.bfloat16)
        place = rem(iota((positions, all_rows), 0), seg_length).astype(jnp.float32)
        source = iota((positions, listed), 1)
        wanted = div(iota((positions, listed), 0), seg_length) * keep
        bias = jnp.full((positions, all_rows), -1e30, jnp.float32)
        for j in range(keep):
            pick = jnp.where(source == wanted + j, 1.0, 0.0).astype(jnp.bfloat16)
            here = jnp.dot(pick, valid, preferred_element_type=jnp.float32)
            bias = jnp.where(here == place, 0.0, bias)
        bias_ref[...] = bias.T

    query = query_ref[...].reshape(rows, group, head_dim)
    keys = cache_ref[:, 0, :, :head_dim]
    values = cache_ref[:, 0, :, head_dim:]
    fresh = fresh_ref[...].astype(jnp.float32)
    scores = jnp.einsum("rgd,rpd->rgp", query, keys, preferred_element_type=jnp.float32) * scale
    bias = bias_ref[pl.ds(pl.multiple_of(step * rows, rows), rows), :]
    scores = scores + bias[:, None, :]
    own = jnp.sum(
        query.astype(jnp.float32) * fresh[:, None, :head_dim], axis=-1, keepdims=True
    ) * scale
    top = jnp.maximum(jnp.max(scores, axis=-1, keepdims=True), own)
    probs = jnp.exp(scores - top).astype(jnp.bfloat16)
    take_new = jnp.exp(own - top)
    denom = jnp.sum(probs.astype(jnp.float32), axis=-1, keepdims=True) + take_new
    numer = jnp.einsum("rgp,rpd->rgd", probs, values, preferred_element_type=jnp.float32)
    numer = numer + take_new * fresh[:, None, head_dim:]
    out_ref[...] = (numer / denom).astype(jnp.bfloat16).reshape(rows, group * head_dim)


def attention(slots, counts, queries, cache_pairs, fresh):
    rows, width = queries.shape
    block = min(ATT_BLOCK, rows)
    return pl.pallas_call(
        attention_body,
        grid=(rows // block,),
        in_specs=[
            pl.BlockSpec(slots.shape, lambda i: (0, 0)),
            pl.BlockSpec(counts.shape, lambda i: (0, 0)),
            pl.BlockSpec((block, width), lambda i: (i, 0)),
            pl.BlockSpec((block,) + cache_pairs.shape[1:], lambda i: (i, 0, 0, 0)),
            pl.BlockSpec((block, fresh.shape[1]), lambda i: (i, 0)),
        ],
        out_specs=pl.BlockSpec((block, width), lambda i: (i, 0)),
        out_shape=jax.ShapeDtypeStruct((rows, width), jnp.bfloat16),
        scratch_shapes=[pltpu.VMEM((rows, cache_pairs.shape[2]), jnp.float32)],
        name="attention",
    )(slots, counts, queries, cache_pairs, fresh)


def project_body(seq_ref, *refs):
    *head_refs, weight_ref, out_ref = refs
    count = len(head_refs)
    weight = weight_ref[...]
    for step, head_ref in zip(STEPS, head_refs):
        part = jnp.dot(head_ref[...], weight, preferred_element_type=jnp.float32)
        out_ref[(seq_ref[0] + (count - step)) & (count - 1)] = part.astype(jnp.bfloat16)


def project(seq, blocks, weight):
    rows = blocks[0].shape[0]
    return pl.pallas_call(
        project_body,
        in_specs=[pl.BlockSpec(memory_space=pltpu.SMEM)]
        + [pl.BlockSpec(memory_space=pltpu.VMEM)] * (len(blocks) + 1),
        out_shape=jax.ShapeDtypeStruct((len(blocks), rows, weight.shape[1]), jnp.bfloat16),
        name="project",
    )(seq, *blocks, weight)


def norm_body(parts_ref, stream_ref, gain_ref, routes_ref, codes_ref, residual_ref, payload_ref):
    seqs, heads, rows, width = parts_ref.shape
    wide = seqs * width
    total = jnp.zeros((rows, 1), jnp.float32)
    for s in range(seqs):
        at = slice(s * width, (s + 1) * width)
        attn = parts_ref[s, 0].astype(jnp.float32)
        for h in range(1, heads):
            attn = attn + parts_ref[s, h].astype(jnp.float32)
        residual = (stream_ref[:, at].astype(jnp.float32) + attn).astype(jnp.bfloat16)
        residual_ref[:, at] = residual
        widened = residual.astype(jnp.float32)
        total = total + jnp.sum(widened * widened, axis=-1, keepdims=True)
    factor = lax.rsqrt(total / wide + epsilon)
    for s in range(seqs):
        at = slice(s * width, (s + 1) * width)
        widened = residual_ref[:, at].astype(jnp.float32)
        payload_ref[:, at] = (widened * factor * gain_ref[:, at]).astype(jnp.bfloat16)
    top = routes_ref.shape[0]
    tail = jnp.concatenate(
        [
            routes_ref[...].astype(jnp.float32),
            codes_ref[...].astype(jnp.float32),
            jnp.zeros((LANES - 2 * top, rows), jnp.float32),
        ],
        axis=0,
    )
    payload_ref[:, wide:] = tail.T.astype(jnp.bfloat16)


def norm(parts, stream, gain, routes, codes):
    rows, wide = stream.shape
    return pl.pallas_call(
        norm_body,
        out_shape=[
            jax.ShapeDtypeStruct((rows, wide), jnp.bfloat16),
            jax.ShapeDtypeStruct((rows, wide + LANES), jnp.bfloat16),
        ],
        name="norm",
    )(parts, stream, gain, routes, codes)


def placement(tail, zh, blocks, top, experts_shape, capacity):
    seqs, zs, ys = experts_shape
    tokens = tail.shape[0]
    rows = tokens // blocks
    experts = seqs * ys
    slots = experts * blocks * capacity
    column = iota((tokens, experts), 1)
    name = (div(column, ys) * zs + zh) * ys + rem(column, ys)
    name = name.astype(jnp.float32)
    match = jnp.zeros((tokens, experts), jnp.float32)
    code = jnp.zeros((tokens, experts), jnp.float32)
    for k in range(top):
        hit = tail[:, k : k + 1] == name
        match = jnp.where(hit, 1.0, match)
        code = jnp.where(hit, tail[:, top + k : top + k + 1], code)
    row, col = iota((tokens, tokens), 0), iota((tokens, tokens), 1)
    before = jnp.where((div(row, rows) == div(col, rows)) & (col < row), 1.0, 0.0)
    rank = jnp.dot(
        before.astype(jnp.bfloat16), match.astype(jnp.bfloat16), preferred_element_type=jnp.float32
    )
    rank = jnp.where(match > 0.0, rank, 99.0)
    spread = jnp.where(
        div(iota((experts, slots), 1), blocks * capacity) == iota((experts, slots), 0), 1.0, 0.0
    ).astype(jnp.bfloat16)
    rank = jnp.dot(rank.astype(jnp.bfloat16), spread, preferred_element_type=jnp.float32)
    code = jnp.dot(code.astype(jnp.bfloat16), spread, preferred_element_type=jnp.float32)
    slot = rem(iota((tokens, slots), 1), blocks * capacity)
    at = div(iota((tokens, slots), 0), rows) * capacity + rank.astype(jnp.int32)
    return jnp.where((slot == at) & (rank < capacity), code, 0.0)


def dispatch_body(zh_ref, *refs, top, experts_shape, capacity):
    *payload_refs, out_ref = refs
    blocks = len(payload_refs)
    wide = out_ref.shape[1]
    tail = jnp.concatenate([r[:, wide:].astype(jnp.float32) for r in payload_refs], axis=0)
    code = placement(tail, zh_ref[0], blocks, top, experts_shape, capacity)
    place = jnp.where(code > 0.0, 1.0, 0.0).T.astype(jnp.bfloat16)
    tokens = jnp.concatenate([r[:, :wide] for r in payload_refs], axis=0)
    out_ref[...] = jnp.dot(place, tokens, preferred_element_type=jnp.float32).astype(jnp.bfloat16)


def dispatch(zh, payloads, wide, static):
    seqs, _, ys = static["experts_shape"]
    slots = seqs * ys * len(payloads) * static["capacity"]
    out = pl.pallas_call(
        lambda *refs: dispatch_body(*refs, **static),
        in_specs=[pl.BlockSpec(memory_space=pltpu.SMEM)]
        + [pl.BlockSpec(memory_space=pltpu.VMEM)] * len(payloads),
        out_shape=jax.ShapeDtypeStruct((slots, wide), jnp.bfloat16),
        name="dispatch",
    )(zh, *payloads)
    return out.reshape(seqs * ys, -1, wide)


def expert_body(rows_ref, gate_ref, up_ref, down_ref, out_ref, acc_ref):
    step = pl.program_id(0)
    rows = rows_ref[...]
    gate = jnp.dot(rows, gate_ref[0], preferred_element_type=jnp.float32)
    up = jnp.dot(rows, up_ref[0], preferred_element_type=jnp.float32)
    act = (gate / (1.0 + jnp.exp(-gate)) * up).astype(jnp.bfloat16)
    part = jnp.dot(act, down_ref[0], preferred_element_type=jnp.float32)
    last = pl.num_programs(0) - 1

    @pl.when(step == 0)
    def _():
        acc_ref[...] = part

    @pl.when((step > 0) & (step < last))
    def _():
        acc_ref[...] += part

    @pl.when(step == last)
    def _():
        out_ref[...] = (acc_ref[...] + part).astype(jnp.bfloat16)


def expert(arrived, gate_weight, up_weight, down_weight):
    shape = arrived.shape
    wide = shape[-1]
    rows = shape[0] * shape[1]
    hidden = gate_weight.shape[2]
    out = pl.pallas_call(
        expert_body,
        grid=(hidden // HID_BLOCK,),
        in_specs=[
            pl.BlockSpec((rows, wide), lambda i: (0, 0)),
            pl.BlockSpec((1, wide, HID_BLOCK), lambda i: (0, 0, i)),
            pl.BlockSpec((1, wide, HID_BLOCK), lambda i: (0, 0, i)),
            pl.BlockSpec((1, HID_BLOCK, wide), lambda i: (0, i, 0)),
        ],
        out_specs=pl.BlockSpec((rows, wide), lambda i: (0, 0)),
        out_shape=jax.ShapeDtypeStruct((rows, wide), jnp.bfloat16),
        scratch_shapes=[pltpu.VMEM((rows, wide), jnp.float32)],
        name="expert",
    )(arrived.reshape(rows, wide), gate_weight, up_weight, down_weight)
    return out.reshape(shape)


def mixed(zh_ref, tail, returned, blocks, static):
    top = static["top"]
    code = placement(tail, zh_ref[0], blocks, **static)
    total = jnp.sum(
        jnp.where(
            (iota(tail.shape, 1) >= top) & (iota(tail.shape, 1) < 2 * top), tail, 0.0
        ),
        axis=-1,
        keepdims=True,
    )
    part = jnp.dot(code.astype(jnp.bfloat16), returned, preferred_element_type=jnp.float32)
    return part / total


def combine_body(zh_ref, *refs, static):
    *tail_refs, returned_ref, o0_ref, o1_ref, o2_ref = refs
    outs = (o0_ref, o1_ref, o2_ref)
    tail = jnp.concatenate([r[...].astype(jnp.float32) for r in tail_refs], axis=0)
    part = mixed(zh_ref, tail, returned_ref[...], len(tail_refs), static)
    rows = part.shape[0] // len(tail_refs)
    for b, out_ref in enumerate(outs):
        out_ref[...] = part[b * rows : (b + 1) * rows].astype(jnp.bfloat16)


def tail_spec(payload):
    rows, wide = payload.shape
    return pl.BlockSpec((rows, LANES), lambda i: (0, wide // LANES - 1))


def combine(zh, payloads, returned, static):
    wide = returned.shape[-1]
    rows = payloads[0].shape[0]
    returned = returned.reshape(-1, wide)
    return pl.pallas_call(
        lambda *refs: combine_body(*refs, static=static),
        grid=(1,),
        in_specs=[pl.BlockSpec(memory_space=pltpu.SMEM)]
        + [tail_spec(p) for p in payloads]
        + [pl.BlockSpec(returned.shape, lambda i: (0, 0))],
        out_specs=[pl.BlockSpec((rows, wide), lambda i: (0, 0))] * len(payloads),
        out_shape=[jax.ShapeDtypeStruct((rows, wide), jnp.bfloat16)] * len(payloads),
        name="combine",
    )(zh, *payloads, returned)


def finish_body(zh_ref, tail_ref, returned_ref, residual_ref, a_ref, b_ref, c_ref, out_ref, *, static):
    tail = tail_ref[...].astype(jnp.float32)
    part = mixed(zh_ref, tail, returned_ref[...], 1, static)
    for ref in (a_ref, b_ref, c_ref, residual_ref):
        part = part + ref[...].astype(jnp.float32)
    out_ref[...] = part.astype(jnp.bfloat16)


def finish(zh, payload, returned, residual, others, static):
    rows, wide = residual.shape
    returned = returned.reshape(-1, wide)
    row_spec = pl.BlockSpec((rows, wide), lambda i: (0, 0))
    return pl.pallas_call(
        lambda *refs: finish_body(*refs, static=static),
        grid=(1,),
        in_specs=[
            pl.BlockSpec(memory_space=pltpu.SMEM),
            tail_spec(payload),
            pl.BlockSpec(returned.shape, lambda i: (0, 0)),
        ]
        + [row_spec] * 4,
        out_specs=row_spec,
        out_shape=jax.ShapeDtypeStruct((rows, wide), jnp.bfloat16),
        name="finish",
    )(zh, payload, returned, residual, *others)


def shift(size, by):
    return [(i, (i + by) % size) for i in range(size)]


def exchange(blocks, axes):
    return lax.all_to_all(blocks, axes, split_axis=0, concat_axis=0, tiled=True)


def on_device(
    stream,
    queries,
    cache_pairs,
    fresh_pairs,
    kept_slots,
    segment_kept_count,
    output_weight,
    norm_gain,
    routes,
    gate_codes,
    gate_weight,
    up_weight,
    down_weight,
):
    rows, wide = stream.shape
    seqs, zs, ys = (lax.axis_size(a) for a in ("seq", "zh", "y"))
    seq = lax.axis_index("seq").astype(jnp.int32).reshape(1)
    zh = lax.axis_index("zh").astype(jnp.int32).reshape(1)
    experts = seqs * zs * ys
    static = dict(
        top=routes.shape[1],
        experts_shape=(seqs, zs, ys),
        capacity=min(rows, max(2, 2 * rows * routes.shape[1] // experts)),
    )

    head_out = attention(
        kept_slots[:, 0].T, segment_kept_count[:, 0].T, queries, cache_pairs, fresh_pairs[:, 0]
    )
    head_blocks = [head_out] + [
        lax.ppermute(head_out, "seq", shift(seqs, d)) for d in STEPS[1:]
    ]
    parts = project(seq, head_blocks, output_weight)
    parts = exchange(parts.reshape(-1, rows, parts.shape[-1]), ("seq",) + HEADS)
    parts = parts.reshape(seqs, -1, rows, parts.shape[-1])
    residual, payload = norm(parts, stream, norm_gain.reshape(1, -1), routes.T, gate_codes.T)

    far = [lax.ppermute(payload, "zh", shift(zs, d)) for d in STEPS[1:]]
    near_rows = exchange(dispatch(zh, [payload], wide, static), PLANE)
    far_rows = exchange(dispatch(zh, far, wide, static), PLANE)
    near_out = expert(near_rows, gate_weight, up_weight, down_weight)
    far_out = exchange(expert(far_rows, gate_weight, up_weight, down_weight), PLANE)
    sums = combine(zh, far, far_out, static)
    others = [lax.ppermute(s, "zh", shift(zs, -d)) for s, d in zip(sums, STEPS[1:])]
    near_out = exchange(near_out, PLANE)
    return finish(zh, payload, near_out, residual, others, static)


def solution(mesh):
    fine = Mesh(mesh.devices.reshape(2, 2, mesh.shape["seq"], 4, 4), MESH_AXES)
    heads, req = HEADS, ("zh", "y")
    tokens = P(req + ("seq",) + heads, None)
    requests = req + ("seq",)
    owned = P(("seq",) + req, None, None)
    placed = (
        tokens,
        P(requests, heads),
        P(requests, heads, None, None),
        P(requests, heads, None),
        P(requests, heads, None),
        P(requests, heads, None),
        P(heads, "seq"),
        P(),
        tokens,
        tokens,
        owned,
        owned,
        owned,
    )
    return jax.shard_map(
        on_device, mesh=fine, in_specs=placed, out_specs=tokens, check_vma=False
    )
```

```python
import jax
import jax.numpy as jnp
from jax import lax
from jax.experimental import pallas as pl
from jax.experimental.pallas import tpu as pltpu
from jax.sharding import Mesh
from jax.sharding import PartitionSpec as P

epsilon = 1e-06
LANES = 128
ATT_BLOCK = 32
MESH_AXES = ("zl", "core", "seq", "zh", "y")
PLANE = ("seq", "y")
HEADS = ("zl", "core")
STEPS = (0, 1, 3, 2)


def grant(mib):
    return pltpu.CompilerParams(vmem_limit_bytes=mib * 2**20)


def in_hbm(*arrays):
    return [pltpu.with_memory_space_constraint(a, pltpu.HBM) for a in arrays]


def iota(shape, dim):
    return lax.broadcasted_iota(jnp.int32, shape, dim)


def div(a, b):
    return lax.div(a, jnp.full_like(a, b))


def rem(a, b):
    return lax.rem(a, jnp.full_like(a, b))


def attention_body(slots_ref, counts_ref, query_ref, cache_ref, fresh_ref, out_ref, bias_ref):
    rows, _, positions, pair = cache_ref.shape
    head_dim = pair // 2
    group = query_ref.shape[1] // head_dim
    scale = head_dim ** (-0.5)
    step = pl.program_id(0)

    @pl.when(step == 0)
    def _():
        listed, all_rows = slots_ref.shape
        segments = counts_ref.shape[0]
        keep = listed // segments
        seg_length = positions // segments
        counts = counts_ref[...].astype(jnp.float32)
        limit = jnp.concatenate(
            [jnp.broadcast_to(counts[s : s + 1], (keep, all_rows)) for s in range(segments)], axis=0
        )
        rank = rem(iota((listed, all_rows), 0), keep).astype(jnp.float32)
        valid = jnp.where(rank < limit, slots_ref[...].astype(jnp.float32), 99.0)
        valid = valid.astype(jnp.bfloat16)
        place = rem(iota((positions, all_rows), 0), seg_length).astype(jnp.float32)
        source = iota((positions, listed), 1)
        wanted = div(iota((positions, listed), 0), seg_length) * keep
        bias = jnp.full((positions, all_rows), -1e30, jnp.float32)
        for j in range(keep):
            pick = jnp.where(source == wanted + j, 1.0, 0.0).astype(jnp.bfloat16)
            here = jnp.dot(pick, valid, preferred_element_type=jnp.float32)
            bias = jnp.where(here == place, 0.0, bias)
        bias_ref[...] = bias.T

    query = query_ref[...].reshape(rows, group, head_dim)
    keys = cache_ref[:, 0, :, :head_dim]
    values = cache_ref[:, 0, :, head_dim:]
    fresh = fresh_ref[...].astype(jnp.float32)
    scores = jnp.einsum("rgd,rpd->rgp", query, keys, preferred_element_type=jnp.float32) * scale
    bias = bias_ref[pl.ds(pl.multiple_of(step * rows, rows), rows), :]
    scores = scores + bias[:, None, :]
    own = jnp.sum(
        query.astype(jnp.float32) * fresh[:, None, :head_dim], axis=-1, keepdims=True
    ) * scale
    top = jnp.maximum(jnp.max(scores, axis=-1, keepdims=True), own)
    probs = jnp.exp(scores - top).astype(jnp.bfloat16)
    take_new = jnp.exp(own - top)
    denom = jnp.sum(probs.astype(jnp.float32), axis=-1, keepdims=True) + take_new
    numer = jnp.einsum("rgp,rpd->rgd", probs, values, preferred_element_type=jnp.float32)
    numer = numer + take_new * fresh[:, None, head_dim:]
    out_ref[...] = (numer / denom).astype(jnp.bfloat16).reshape(rows, group * head_dim)


def attention(slots, counts, queries, cache_pairs, fresh):
    rows, width = queries.shape
    block = min(ATT_BLOCK, rows)
    return pl.pallas_call(
        attention_body,
        grid=(rows // block,),
        in_specs=[
            pl.BlockSpec(slots.shape, lambda i: (0, 0)),
            pl.BlockSpec(counts.shape, lambda i: (0, 0)),
            pl.BlockSpec((block, width), lambda i: (i, 0)),
            pl.BlockSpec((block,) + cache_pairs.shape[1:], lambda i: (i, 0, 0, 0)),
            pl.BlockSpec((block, fresh.shape[1]), lambda i: (i, 0)),
        ],
        out_specs=pl.BlockSpec((block, width), lambda i: (i, 0)),
        out_shape=jax.ShapeDtypeStruct((rows, width), jnp.bfloat16),
        scratch_shapes=[pltpu.VMEM((rows, cache_pairs.shape[2]), jnp.float32)],
        compiler_params=grant(24),
        name="attention",
    )(*in_hbm(slots, counts, queries, cache_pairs, fresh))


def project_body(seq_ref, *refs):
    *head_refs, weight_ref, out_ref = refs
    count = len(head_refs)
    weight = weight_ref[...]
    for step, head_ref in zip(STEPS, head_refs):
        part = jnp.dot(head_ref[...], weight, preferred_element_type=jnp.float32)
        out_ref[(seq_ref[0] + (count - step)) & (count - 1)] = part.astype(jnp.bfloat16)


def project(seq, blocks, weight):
    rows = blocks[0].shape[0]
    return pl.pallas_call(
        project_body,
        in_specs=[pl.BlockSpec(memory_space=pltpu.SMEM)]
        + [pl.BlockSpec(memory_space=pltpu.VMEM)] * (len(blocks) + 1),
        out_shape=jax.ShapeDtypeStruct((len(blocks), rows, weight.shape[1]), jnp.bfloat16),
        compiler_params=grant(12),
        name="project",
    )(seq, *blocks, weight)


def norm_body(parts_ref, stream_ref, gain_ref, routes_ref, codes_ref, residual_ref, payload_ref):
    seqs, heads, rows, width = parts_ref.shape
    wide = seqs * width
    total = jnp.zeros((rows, 1), jnp.float32)
    for s in range(seqs):
        at = slice(s * width, (s + 1) * width)
        attn = parts_ref[s, 0].astype(jnp.float32)
        for h in range(1, heads):
            attn = attn + parts_ref[s, h].astype(jnp.float32)
        residual = (stream_ref[:, at].astype(jnp.float32) + attn).astype(jnp.bfloat16)
        residual_ref[:, at] = residual
        widened = residual.astype(jnp.float32)
        total = total + jnp.sum(widened * widened, axis=-1, keepdims=True)
    factor = lax.rsqrt(total / wide + epsilon)
    for s in range(seqs):
        at = slice(s * width, (s + 1) * width)
        widened = residual_ref[:, at].astype(jnp.float32)
        normed = (widened * factor * gain_ref[:, at]).astype(jnp.bfloat16)
        for z in range(payload_ref.shape[0]):
            payload_ref[z, :, at] = normed
    top = routes_ref.shape[0]
    tail = jnp.concatenate(
        [
            routes_ref[...].astype(jnp.float32),
            codes_ref[...].astype(jnp.float32),
            jnp.zeros((LANES - 2 * top, rows), jnp.float32),
        ],
        axis=0,
    )
    tail = tail.T.astype(jnp.bfloat16)
    for z in range(payload_ref.shape[0]):
        payload_ref[z, :, wide:] = tail


def norm(parts, stream, gain, routes, codes, copies):
    rows, wide = stream.shape
    return pl.pallas_call(
        norm_body,
        out_shape=[
            jax.ShapeDtypeStruct((rows, wide), jnp.bfloat16),
            pltpu.HBM((copies, rows, wide + LANES), jnp.bfloat16),
        ],
        compiler_params=grant(8),
        name="norm",
    )(parts, stream, gain, routes, codes)


def placement(tail, zh, blocks, top, experts_shape, capacity):
    seqs, zs, ys = experts_shape
    tokens = tail.shape[0]
    rows = tokens // blocks
    experts = seqs * ys
    slots = experts * blocks * capacity
    column = iota((tokens, experts), 1)
    name = (div(column, ys) * zs + zh) * ys + rem(column, ys)
    name = name.astype(jnp.float32)
    match = jnp.zeros((tokens, experts), jnp.float32)
    code = jnp.zeros((tokens, experts), jnp.float32)
    for k in range(top):
        hit = tail[:, k : k + 1] == name
        match = jnp.where(hit, 1.0, match)
        code = jnp.where(hit, tail[:, top + k : top + k + 1], code)
    row, col = iota((tokens, tokens), 0), iota((tokens, tokens), 1)
    before = jnp.where((div(row, rows) == div(col, rows)) & (col < row), 1.0, 0.0)
    rank = jnp.dot(
        before.astype(jnp.bfloat16), match.astype(jnp.bfloat16), preferred_element_type=jnp.float32
    )
    rank = jnp.where(match > 0.0, rank, 99.0)
    spread = jnp.where(
        div(iota((experts, slots), 1), blocks * capacity) == iota((experts, slots), 0), 1.0, 0.0
    ).astype(jnp.bfloat16)
    rank = jnp.dot(rank.astype(jnp.bfloat16), spread, preferred_element_type=jnp.float32)
    code = jnp.dot(code.astype(jnp.bfloat16), spread, preferred_element_type=jnp.float32)
    slot = rem(iota((tokens, slots), 1), blocks * capacity)
    at = div(iota((tokens, slots), 0), rows) * capacity + rank.astype(jnp.int32)
    return jnp.where((slot == at) & (rank < capacity), code, 0.0)


def dispatch_body(zh_ref, payload_ref, out_ref, code_ref, total_ref, *, steps, static):
    planes, rows, _ = payload_ref.shape
    wide = out_ref.shape[1]
    top = static["top"]
    ats = [(zh_ref[0] + (planes - d)) & (planes - 1) for d in steps]
    tail = jnp.concatenate([payload_ref[at, :, wide:].astype(jnp.float32) for at in ats], axis=0)
    code = placement(tail, zh_ref[0], len(steps), **static)
    place = jnp.where(code > 0.0, 1.0, 0.0).T.astype(jnp.bfloat16)
    tokens = jnp.concatenate([payload_ref[at, :, :wide] for at in ats], axis=0)
    out_ref[...] = jnp.dot(place, tokens, preferred_element_type=jnp.float32).astype(jnp.bfloat16)
    code_ref[...] = code.astype(jnp.bfloat16)
    lane = iota(tail.shape, 1)
    listed = jnp.where((lane >= top) & (lane < 2 * top), tail, 0.0)
    total_ref[...] = jnp.broadcast_to(jnp.sum(listed, axis=-1, keepdims=True), tail.shape)


def dispatch(zh, payload, steps, static):
    seqs, _, ys = static["experts_shape"]
    rows, wide = payload.shape[1], payload.shape[2] - LANES
    tokens, slots = rows * len(steps), seqs * ys * len(steps) * static["capacity"]
    out, code, total = pl.pallas_call(
        lambda *refs: dispatch_body(*refs, steps=steps, static=static),
        in_specs=[
            pl.BlockSpec(memory_space=pltpu.SMEM),
            pl.BlockSpec(memory_space=pltpu.VMEM),
        ],
        out_shape=[
            pltpu.HBM((slots, wide), jnp.bfloat16),
            jax.ShapeDtypeStruct((tokens, slots), jnp.bfloat16),
            jax.ShapeDtypeStruct((tokens, LANES), jnp.float32),
        ],
        compiler_params=grant(12),
        name="dispatch",
    )(zh, payload)
    return out.reshape(seqs * ys, -1, wide), (code, total)


def expert_body(rows_ref, gate_ref, up_hbm, down_hbm, out_ref, up_ref, down_ref, sems):
    fetch_up = pltpu.make_async_copy(up_hbm.at[0], up_ref, sems.at[0])
    fetch_down = pltpu.make_async_copy(down_hbm.at[0], down_ref, sems.at[1])
    fetch_up.start()
    fetch_down.start()
    rows = rows_ref[...]
    gate = jnp.dot(rows, gate_ref[0], preferred_element_type=jnp.float32)
    gate = gate / (1.0 + jnp.exp(-gate))
    fetch_up.wait()
    up = jnp.dot(rows, up_ref[...], preferred_element_type=jnp.float32)
    act = (gate * up).astype(jnp.bfloat16)
    fetch_down.wait()
    part = jnp.dot(act, down_ref[...], preferred_element_type=jnp.float32)
    out_ref[...] = part.astype(jnp.bfloat16)


def expert(arrived, gate_weight, up_weight, down_weight):
    shape = arrived.shape
    wide = shape[-1]
    rows = shape[0] * shape[1]
    hidden = gate_weight.shape[2]
    up_weight, down_weight = in_hbm(up_weight, down_weight)
    out = pl.pallas_call(
        expert_body,
        in_specs=[
            pl.BlockSpec(memory_space=pltpu.VMEM),
            pl.BlockSpec(memory_space=pltpu.VMEM),
            pl.BlockSpec(memory_space=pl.ANY),
            pl.BlockSpec(memory_space=pl.ANY),
        ],
        out_shape=pltpu.HBM((rows, wide), jnp.bfloat16),
        scratch_shapes=[
            pltpu.VMEM((wide, hidden), jnp.bfloat16),
            pltpu.VMEM((hidden, wide), jnp.bfloat16),
            pltpu.SemaphoreType.DMA((2,)),
        ],
        compiler_params=grant(30),
        name="expert",
    )(arrived.reshape(rows, wide), gate_weight, up_weight, down_weight)
    return out.reshape(shape)


def mixed(code_ref, total_ref, returned_ref):
    part = jnp.dot(code_ref[...], returned_ref[...], preferred_element_type=jnp.float32)
    return part / total_ref[:, :1]


def combine_body(code_ref, total_ref, returned_ref, *outs):
    part = mixed(code_ref, total_ref, returned_ref)
    rows = part.shape[0] // len(outs)
    for b, out_ref in enumerate(outs):
        out_ref[...] = part[b * rows : (b + 1) * rows].astype(jnp.bfloat16)


def combine(mix, returned, blocks):
    wide = returned.shape[-1]
    rows = mix[0].shape[0] // blocks
    return pl.pallas_call(
        combine_body,
        out_shape=[jax.ShapeDtypeStruct((rows, wide), jnp.bfloat16)] * blocks,
        compiler_params=grant(8),
        name="combine",
    )(*mix, returned.reshape(-1, wide))


def finish_body(code_ref, total_ref, returned_ref, *refs):
    *more, out_ref = refs
    part = mixed(code_ref, total_ref, returned_ref)
    for ref in more:
        part = part + ref[...].astype(jnp.float32)
    out_ref[...] = part.astype(jnp.bfloat16)


def finish(mix, returned, *more):
    wide = returned.shape[-1]
    return pl.pallas_call(
        finish_body,
        out_shape=jax.ShapeDtypeStruct(more[0].shape, jnp.bfloat16),
        compiler_params=grant(8),
        name="finish",
    )(*mix, returned.reshape(-1, wide), *more)


def shift(size, by):
    return [(i, (i + by) % size) for i in range(size)]


def exchange(blocks, axes):
    return lax.all_to_all(blocks, axes, split_axis=0, concat_axis=0, tiled=True)


def on_device(
    stream,
    queries,
    cache_pairs,
    fresh_pairs,
    kept_slots,
    segment_kept_count,
    output_weight,
    norm_gain,
    routes,
    gate_codes,
    gate_weight,
    up_weight,
    down_weight,
):
    rows, wide = stream.shape
    seqs, zs, ys = (lax.axis_size(a) for a in ("seq", "zh", "y"))
    seq = lax.axis_index("seq").astype(jnp.int32).reshape(1)
    zh = lax.axis_index("zh").astype(jnp.int32).reshape(1)
    experts = seqs * zs * ys
    static = dict(
        top=routes.shape[1],
        experts_shape=(seqs, zs, ys),
        capacity=min(rows, max(2, 2 * rows * routes.shape[1] // experts)),
    )

    head_out = attention(
        kept_slots[:, 0].T, segment_kept_count[:, 0].T, queries, cache_pairs, fresh_pairs[:, 0]
    )
    head_blocks = [head_out] + [
        lax.ppermute(head_out, "seq", shift(seqs, d)) for d in STEPS[1:]
    ]
    parts = project(seq, head_blocks, output_weight)
    parts = exchange(parts.reshape(-1, rows, parts.shape[-1]), ("seq",) + HEADS)
    parts = parts.reshape(seqs, -1, rows, parts.shape[-1])
    residual, payload = norm(
        parts, stream, norm_gain.reshape(1, -1), routes.T, gate_codes.T, zs
    )
    weights = (gate_weight, up_weight, down_weight)

    gathered = exchange(payload, "zh")
    near_rows, near_mix = dispatch(zh, payload, STEPS[:1], static)
    far_rows, far_mix = dispatch(zh, gathered, STEPS[1:], static)
    near_rows, far_rows = exchange(near_rows, PLANE), exchange(far_rows, PLANE)
    near_out = expert(near_rows, *weights)
    far_out = exchange(expert(far_rows, *weights), PLANE)
    sums = combine(far_mix, far_out, len(STEPS) - 1)
    others = [lax.ppermute(s, "zh", shift(zs, -d)) for s, d in zip(sums, STEPS[1:])]
    near_out = exchange(near_out, PLANE)
    return finish(near_mix, near_out, residual, *others)


def solution(mesh):
    fine = Mesh(mesh.devices.reshape(2, 2, mesh.shape["seq"], 4, 4), MESH_AXES)
    heads, req = HEADS, ("zh", "y")
    tokens = P(req + ("seq",) + heads, None)
    requests = req + ("seq",)
    owned = P(("seq",) + req, None, None)
    placed = (
        tokens,
        P(requests, heads),
        P(requests, heads, None, None),
        P(requests, heads, None),
        P(requests, heads, None),
        P(requests, heads, None),
        P(heads, "seq"),
        P(),
        tokens,
        tokens,
        owned,
        owned,
        owned,
    )
    return jax.shard_map(
        on_device, mesh=fine, in_specs=placed, out_specs=tokens, check_vma=False
    )
```

```python
import jax
import jax.numpy as jnp
from jax import lax
from jax.experimental import pallas as pl
from jax.experimental.pallas import tpu as pltpu
from jax.sharding import Mesh
from jax.sharding import PartitionSpec as P

epsilon = 1e-06
LANES = 128
ATT_BLOCK = 32
MESH_AXES = ("zl", "core", "seq", "zh", "y")
PLANE = ("seq", "y")
HEADS = ("zl", "core")
STEPS = (0, 1, 3, 2)


def grant(mib):
    return pltpu.CompilerParams(vmem_limit_bytes=mib * 2**20)


def in_hbm(*arrays):
    return [pltpu.with_memory_space_constraint(a, pltpu.HBM) for a in arrays]


def iota(shape, dim):
    return lax.broadcasted_iota(jnp.int32, shape, dim)


def div(a, b):
    return lax.div(a, jnp.full_like(a, b))


def rem(a, b):
    return lax.rem(a, jnp.full_like(a, b))


def attention_body(slots_ref, counts_ref, query_ref, cache_ref, fresh_ref, out_ref, bias_ref):
    rows, _, positions, pair = cache_ref.shape
    head_dim = pair // 2
    group = query_ref.shape[1] // head_dim
    scale = head_dim ** (-0.5)
    step = pl.program_id(0)

    @pl.when(step == 0)
    def _():
        listed, all_rows = slots_ref.shape
        segments = counts_ref.shape[0]
        keep = listed // segments
        seg_length = positions // segments
        counts = counts_ref[...].astype(jnp.float32)
        limit = jnp.concatenate(
            [jnp.broadcast_to(counts[s : s + 1], (keep, all_rows)) for s in range(segments)], axis=0
        )
        rank = rem(iota((listed, all_rows), 0), keep).astype(jnp.float32)
        valid = jnp.where(rank < limit, slots_ref[...].astype(jnp.float32), 99.0)
        valid = valid.astype(jnp.bfloat16)
        place = rem(iota((positions, all_rows), 0), seg_length).astype(jnp.float32)
        source = iota((positions, listed), 1)
        wanted = div(iota((positions, listed), 0), seg_length) * keep
        bias = jnp.full((positions, all_rows), -1e30, jnp.float32)
        for j in range(keep):
            pick = jnp.where(source == wanted + j, 1.0, 0.0).astype(jnp.bfloat16)
            here = jnp.dot(pick, valid, preferred_element_type=jnp.float32)
            bias = jnp.where(here == place, 0.0, bias)
        bias_ref[...] = bias.T

    query = query_ref[...].reshape(rows, group, head_dim)
    keys = cache_ref[:, 0, :, :head_dim]
    values = cache_ref[:, 0, :, head_dim:]
    fresh = fresh_ref[...].astype(jnp.float32)
    scores = jnp.einsum("rgd,rpd->rgp", query, keys, preferred_element_type=jnp.float32) * scale
    bias = bias_ref[pl.ds(pl.multiple_of(step * rows, rows), rows), :]
    scores = scores + bias[:, None, :]
    own = jnp.sum(
        query.astype(jnp.float32) * fresh[:, None, :head_dim], axis=-1, keepdims=True
    ) * scale
    top = jnp.maximum(jnp.max(scores, axis=-1, keepdims=True), own)
    probs = jnp.exp(scores - top).astype(jnp.bfloat16)
    take_new = jnp.exp(own - top)
    denom = jnp.sum(probs.astype(jnp.float32), axis=-1, keepdims=True) + take_new
    numer = jnp.einsum("rgp,rpd->rgd", probs, values, preferred_element_type=jnp.float32)
    numer = numer + take_new * fresh[:, None, head_dim:]
    out_ref[...] = (numer / denom).astype(jnp.bfloat16).reshape(rows, group * head_dim)


def attention(slots, counts, queries, cache_pairs, fresh):
    rows, width = queries.shape
    block = min(ATT_BLOCK, rows)
    return pl.pallas_call(
        attention_body,
        grid=(rows // block,),
        in_specs=[
            pl.BlockSpec(slots.shape, lambda i: (0, 0)),
            pl.BlockSpec(counts.shape, lambda i: (0, 0)),
            pl.BlockSpec((block, width), lambda i: (i, 0)),
            pl.BlockSpec((block,) + cache_pairs.shape[1:], lambda i: (i, 0, 0, 0)),
            pl.BlockSpec((block, fresh.shape[1]), lambda i: (i, 0)),
        ],
        out_specs=pl.BlockSpec((block, width), lambda i: (i, 0)),
        out_shape=jax.ShapeDtypeStruct((rows, width), jnp.bfloat16),
        scratch_shapes=[pltpu.VMEM((rows, cache_pairs.shape[2]), jnp.float32)],
        compiler_params=grant(24),
        name="attention",
    )(*in_hbm(slots, counts, queries, cache_pairs, fresh))


def project_body(here_ref, *refs):
    *head_refs, weight_ref, out_ref = refs
    count = len(head_refs)
    weight = weight_ref[...]
    for step, head_ref in zip(STEPS, head_refs):
        part = jnp.dot(head_ref[...], weight, preferred_element_type=jnp.float32)
        out_ref[(here_ref[0] + (count - step)) & (count - 1)] = part.astype(jnp.bfloat16)


def project(here, blocks, weight):
    rows = blocks[0].shape[0]
    return pl.pallas_call(
        project_body,
        in_specs=[pl.BlockSpec(memory_space=pltpu.SMEM)]
        + [pl.BlockSpec(memory_space=pltpu.VMEM)] * (len(blocks) + 1),
        out_shape=jax.ShapeDtypeStruct((len(blocks), rows, weight.shape[1]), jnp.bfloat16),
        compiler_params=grant(12),
        name="project",
    )(here, *blocks, weight)


def norm_body(parts_ref, stream_ref, gain_ref, routes_ref, codes_ref, residual_ref, payload_ref):
    seqs, heads, rows, width = parts_ref.shape
    wide = seqs * width
    total = jnp.zeros((rows, 1), jnp.float32)
    for s in range(seqs):
        at = slice(s * width, (s + 1) * width)
        attn = parts_ref[s, 0].astype(jnp.float32)
        for h in range(1, heads):
            attn = attn + parts_ref[s, h].astype(jnp.float32)
        residual = (stream_ref[:, at].astype(jnp.float32) + attn).astype(jnp.bfloat16)
        residual_ref[:, at] = residual
        widened = residual.astype(jnp.float32)
        total = total + jnp.sum(widened * widened, axis=-1, keepdims=True)
    factor = lax.rsqrt(total / wide + epsilon)
    for s in range(seqs):
        at = slice(s * width, (s + 1) * width)
        widened = residual_ref[:, at].astype(jnp.float32)
        normed = (widened * factor * gain_ref[:, at]).astype(jnp.bfloat16)
        for z in range(payload_ref.shape[0]):
            payload_ref[z, :, at] = normed
    top = routes_ref.shape[0]
    tail = jnp.concatenate(
        [
            routes_ref[...].astype(jnp.float32),
            codes_ref[...].astype(jnp.float32),
            jnp.zeros((LANES - 2 * top, rows), jnp.float32),
        ],
        axis=0,
    )
    tail = tail.T.astype(jnp.bfloat16)
    for z in range(payload_ref.shape[0]):
        payload_ref[z, :, wide:] = tail


def norm(parts, stream, gain, routes, codes, copies):
    rows, wide = stream.shape
    return pl.pallas_call(
        norm_body,
        out_shape=[
            jax.ShapeDtypeStruct((rows, wide), jnp.bfloat16),
            jax.ShapeDtypeStruct((copies, rows, wide + LANES), jnp.bfloat16),
        ],
        compiler_params=grant(8),
        name="norm",
    )(parts, stream, gain, routes, codes)


def placement(tail, zh, blocks, top, experts_shape, capacity):
    seqs, zs, ys = experts_shape
    tokens = tail.shape[0]
    rows = tokens // blocks
    experts = seqs * ys
    slots = experts * blocks * capacity
    column = iota((tokens, experts), 1)
    name = (div(column, ys) * zs + zh) * ys + rem(column, ys)
    name = name.astype(jnp.float32)
    match = jnp.zeros((tokens, experts), jnp.float32)
    code = jnp.zeros((tokens, experts), jnp.float32)
    for k in range(top):
        hit = tail[:, k : k + 1] == name
        match = jnp.where(hit, 1.0, match)
        code = jnp.where(hit, tail[:, top + k : top + k + 1], code)
    row, col = iota((tokens, tokens), 0), iota((tokens, tokens), 1)
    before = jnp.where((div(row, rows) == div(col, rows)) & (col < row), 1.0, 0.0)
    rank = jnp.dot(
        before.astype(jnp.bfloat16), match.astype(jnp.bfloat16), preferred_element_type=jnp.float32
    )
    rank = jnp.where(match > 0.0, rank, 99.0)
    spread = jnp.where(
        div(iota((experts, slots), 1), blocks * capacity) == iota((experts, slots), 0), 1.0, 0.0
    ).astype(jnp.bfloat16)
    rank = jnp.dot(rank.astype(jnp.bfloat16), spread, preferred_element_type=jnp.float32)
    code = jnp.dot(code.astype(jnp.bfloat16), spread, preferred_element_type=jnp.float32)
    slot = rem(iota((tokens, slots), 1), blocks * capacity)
    at = div(iota((tokens, slots), 0), rows) * capacity + rank.astype(jnp.int32)
    return jnp.where((slot == at) & (rank < capacity), code, 0.0)


def dispatch_body(here_ref, payload_ref, out_ref, code_ref, total_ref, *, static):
    planes, rows, _ = payload_ref.shape
    wide = out_ref.shape[1]
    top = static["top"]
    tail = jnp.concatenate(
        [payload_ref[z, :, wide:].astype(jnp.float32) for z in range(planes)], axis=0
    )
    code = placement(tail, here_ref[1], planes, **static)
    place = jnp.where(code > 0.0, 1.0, 0.0).T.astype(jnp.bfloat16)
    tokens = jnp.concatenate([payload_ref[z, :, :wide] for z in range(planes)], axis=0)
    out_ref[...] = jnp.dot(place, tokens, preferred_element_type=jnp.float32).astype(jnp.bfloat16)
    code_ref[...] = code.astype(jnp.bfloat16)
    lane = iota(tail.shape, 1)
    listed = jnp.where((lane >= top) & (lane < 2 * top), tail, 0.0)
    total_ref[...] = jnp.broadcast_to(jnp.sum(listed, axis=-1, keepdims=True), tail.shape)


def dispatch(here, payload, static):
    seqs, _, ys = static["experts_shape"]
    planes, rows, wide = payload.shape
    wide = wide - LANES
    tokens, slots = planes * rows, seqs * ys * planes * static["capacity"]
    out, code, total = pl.pallas_call(
        lambda *refs: dispatch_body(*refs, static=static),
        in_specs=[
            pl.BlockSpec(memory_space=pltpu.SMEM),
            pl.BlockSpec(memory_space=pltpu.VMEM),
        ],
        out_shape=[
            jax.ShapeDtypeStruct((slots, wide), jnp.bfloat16),
            jax.ShapeDtypeStruct((tokens, slots), jnp.bfloat16),
            jax.ShapeDtypeStruct((tokens, LANES), jnp.float32),
        ],
        compiler_params=grant(16),
        name="dispatch",
    )(here, payload)
    return out.reshape(seqs * ys, -1, wide), (code, total)


def expert_body(rows_ref, gate_ref, up_ref, down_hbm, out_ref, down_ref, sem):
    fetch = pltpu.make_async_copy(down_hbm.at[0], down_ref, sem)
    fetch.start()
    rows = rows_ref[...]
    gate = jnp.dot(rows, gate_ref[0], preferred_element_type=jnp.float32)
    up = jnp.dot(rows, up_ref[0], preferred_element_type=jnp.float32)
    act = (gate / (1.0 + jnp.exp(-gate)) * up).astype(jnp.bfloat16)
    fetch.wait()
    part = jnp.dot(act, down_ref[...], preferred_element_type=jnp.float32)
    out_ref[...] = part.astype(jnp.bfloat16)


def expert(arrived, gate_weight, up_weight, down_weight):
    shape = arrived.shape
    wide = shape[-1]
    rows = shape[0] * shape[1]
    return pl.pallas_call(
        expert_body,
        in_specs=[pl.BlockSpec(memory_space=pltpu.VMEM)] * 3 + [pl.BlockSpec(memory_space=pl.ANY)],
        out_shape=jax.ShapeDtypeStruct((rows, wide), jnp.bfloat16),
        scratch_shapes=[
            pltpu.VMEM(down_weight.shape[1:], jnp.bfloat16),
            pltpu.SemaphoreType.DMA,
        ],
        compiler_params=grant(24),
        name="expert",
    )(
        arrived.reshape(rows, wide),
        pltpu.with_memory_space_constraint(gate_weight, pltpu.VMEM),
        pltpu.with_memory_space_constraint(up_weight, pltpu.VMEM),
        *in_hbm(down_weight),
    ).reshape(shape)


def combine_body(code_ref, total_ref, returned_ref, out_ref):
    part = jnp.dot(code_ref[...], returned_ref[...], preferred_element_type=jnp.float32)
    out_ref[...] = (part / total_ref[:, :1]).astype(jnp.bfloat16)


def combine(code, total, returned, planes):
    wide = returned.shape[-1]
    out = pl.pallas_call(
        combine_body,
        out_shape=jax.ShapeDtypeStruct((code.shape[0], wide), jnp.bfloat16),
        compiler_params=grant(10),
        name="combine",
    )(code, total, returned.reshape(-1, wide))
    return out.reshape(planes, -1, wide)


def finish_body(residual_ref, sums_ref, out_ref):
    part = residual_ref[...].astype(jnp.float32)
    for z in range(sums_ref.shape[0]):
        part = part + sums_ref[z].astype(jnp.float32)
    out_ref[...] = part.astype(jnp.bfloat16)


def finish(residual, sums):
    return pl.pallas_call(
        finish_body,
        out_shape=jax.ShapeDtypeStruct(residual.shape, jnp.bfloat16),
        compiler_params=grant(8),
        name="finish",
    )(residual, sums)


def shift(size, by):
    return [(i, (i + by) % size) for i in range(size)]


def exchange(blocks, axes):
    return lax.all_to_all(blocks, axes, split_axis=0, concat_axis=0, tiled=True)


def on_device(
    stream,
    queries,
    cache_pairs,
    fresh_pairs,
    kept_slots,
    segment_kept_count,
    output_weight,
    norm_gain,
    routes,
    gate_codes,
    gate_weight,
    up_weight,
    down_weight,
):
    rows, wide = stream.shape
    seqs, zs, ys = (lax.axis_size(a) for a in ("seq", "zh", "y"))
    here = jnp.stack([lax.axis_index("seq"), lax.axis_index("zh")]).astype(jnp.int32)
    experts = seqs * zs * ys
    static = dict(
        top=routes.shape[1],
        experts_shape=(seqs, zs, ys),
        capacity=min(rows, max(2, 2 * rows * routes.shape[1] // experts)),
    )

    head_out = attention(
        kept_slots[:, 0].T, segment_kept_count[:, 0].T, queries, cache_pairs, fresh_pairs[:, 0]
    )
    head_blocks = [head_out] + [
        lax.ppermute(head_out, "seq", shift(seqs, d)) for d in STEPS[1:]
    ]
    parts = project(here, head_blocks, output_weight)
    parts = exchange(parts.reshape(-1, rows, parts.shape[-1]), ("seq",) + HEADS)
    parts = parts.reshape(seqs, -1, rows, parts.shape[-1])
    residual, payload = norm(
        parts, stream, norm_gain.reshape(1, -1), routes.T, gate_codes.T, zs
    )
    sent, mix = dispatch(here, exchange(payload, "zh"), static)
    made = expert(exchange(sent, PLANE), gate_weight, up_weight, down_weight)
    sums = combine(*mix, exchange(made, PLANE), zs)
    return finish(residual, exchange(sums, "zh"))


def solution(mesh):
    fine = Mesh(mesh.devices.reshape(2, 2, mesh.shape["seq"], 4, 4), MESH_AXES)
    heads, req = HEADS, ("zh", "y")
    tokens = P(req + ("seq",) + heads, None)
    requests = req + ("seq",)
    owned = P(("seq",) + req, None, None)
    placed = (
        tokens,
        P(requests, heads),
        P(requests, heads, None, None),
        P(requests, heads, None),
        P(requests, heads, None),
        P(requests, heads, None),
        P(heads, "seq"),
        P(),
        tokens,
        tokens,
        owned,
        owned,
        owned,
    )
    return jax.shard_map(
        on_device, mesh=fine, in_specs=placed, out_specs=tokens, check_vma=False
    )
```

```python
import jax
import jax.numpy as jnp
from jax import lax
from jax.experimental import pallas as pl
from jax.experimental.pallas import tpu as pltpu
from jax.sharding import Mesh
from jax.sharding import PartitionSpec as P

epsilon = 1e-06
LANES = 128
ATT_BLOCK = 32
MESH_AXES = ("zl", "core", "seq", "zh", "y")
PLANE = ("seq", "y")
HEADS = ("zl", "core")
STEPS = (0, 1, 3, 2)


def grant(mib):
    return pltpu.CompilerParams(vmem_limit_bytes=mib * 2**20)


def in_hbm(*arrays):
    return [pltpu.with_memory_space_constraint(a, pltpu.HBM) for a in arrays]


def iota(shape, dim):
    return lax.broadcasted_iota(jnp.int32, shape, dim)


def div(a, b):
    return lax.div(a, jnp.full_like(a, b))


def rem(a, b):
    return lax.rem(a, jnp.full_like(a, b))


def attention_body(slots_ref, counts_ref, query_ref, cache_ref, fresh_ref, out_ref, bias_ref):
    rows, _, positions, pair = cache_ref.shape
    head_dim = pair // 2
    group = query_ref.shape[1] // head_dim
    scale = head_dim ** (-0.5)
    step = pl.program_id(0)

    @pl.when(step == 0)
    def _():
        listed, all_rows = slots_ref.shape
        segments = counts_ref.shape[0]
        keep = listed // segments
        seg_length = positions // segments
        counts = counts_ref[...].astype(jnp.float32)
        limit = jnp.concatenate(
            [jnp.broadcast_to(counts[s : s + 1], (keep, all_rows)) for s in range(segments)], axis=0
        )
        rank = rem(iota((listed, all_rows), 0), keep).astype(jnp.float32)
        valid = jnp.where(rank < limit, slots_ref[...].astype(jnp.float32), 99.0)
        valid = valid.astype(jnp.bfloat16)
        place = rem(iota((positions, all_rows), 0), seg_length).astype(jnp.float32)
        source = iota((positions, listed), 1)
        wanted = div(iota((positions, listed), 0), seg_length) * keep
        bias = jnp.full((positions, all_rows), -1e30, jnp.float32)
        for j in range(keep):
            pick = jnp.where(source == wanted + j, 1.0, 0.0).astype(jnp.bfloat16)
            here = jnp.dot(pick, valid, preferred_element_type=jnp.float32)
            bias = jnp.where(here == place, 0.0, bias)
        bias_ref[...] = bias.T

    query = query_ref[...].reshape(rows, group, head_dim)
    keys = cache_ref[:, 0, :, :head_dim]
    values = cache_ref[:, 0, :, head_dim:]
    fresh = fresh_ref[...].astype(jnp.float32)
    scores = jnp.einsum("rgd,rpd->rgp", query, keys, preferred_element_type=jnp.float32) * scale
    bias = bias_ref[pl.ds(pl.multiple_of(step * rows, rows), rows), :]
    scores = scores + bias[:, None, :]
    own = jnp.sum(
        query.astype(jnp.float32) * fresh[:, None, :head_dim], axis=-1, keepdims=True
    ) * scale
    top = jnp.maximum(jnp.max(scores, axis=-1, keepdims=True), own)
    probs = jnp.exp(scores - top).astype(jnp.bfloat16)
    take_new = jnp.exp(own - top)
    denom = jnp.sum(probs.astype(jnp.float32), axis=-1, keepdims=True) + take_new
    numer = jnp.einsum("rgp,rpd->rgd", probs, values, preferred_element_type=jnp.float32)
    numer = numer + take_new * fresh[:, None, head_dim:]
    out_ref[...] = (numer / denom).astype(jnp.bfloat16).reshape(rows, group * head_dim)


def attention(slots, counts, queries, cache_pairs, fresh):
    rows, width = queries.shape
    block = min(ATT_BLOCK, rows)
    return pl.pallas_call(
        attention_body,
        grid=(rows // block,),
        in_specs=[
            pl.BlockSpec(slots.shape, lambda i: (0, 0)),
            pl.BlockSpec(counts.shape, lambda i: (0, 0)),
            pl.BlockSpec((block, width), lambda i: (i, 0)),
            pl.BlockSpec((block,) + cache_pairs.shape[1:], lambda i: (i, 0, 0, 0)),
            pl.BlockSpec((block, fresh.shape[1]), lambda i: (i, 0)),
        ],
        out_specs=pl.BlockSpec((block, width), lambda i: (i, 0)),
        out_shape=jax.ShapeDtypeStruct((rows, width), jnp.bfloat16),
        scratch_shapes=[pltpu.VMEM((rows, cache_pairs.shape[2]), jnp.float32)],
        compiler_params=grant(24),
        name="attention",
    )(*in_hbm(slots, counts, queries, cache_pairs, fresh))


def project_body(here_ref, *refs):
    *head_refs, weight_ref, out_ref = refs
    count = len(head_refs)
    weight = weight_ref[...]
    for step, head_ref in zip(STEPS, head_refs):
        part = jnp.dot(head_ref[...], weight, preferred_element_type=jnp.float32)
        out_ref[(here_ref[0] + (count - step)) & (count - 1)] = part.astype(jnp.bfloat16)


def project(here, blocks, weight):
    rows = blocks[0].shape[0]
    return pl.pallas_call(
        project_body,
        in_specs=[pl.BlockSpec(memory_space=pltpu.SMEM)]
        + [pl.BlockSpec(memory_space=pltpu.VMEM)] * (len(blocks) + 1),
        out_shape=jax.ShapeDtypeStruct((len(blocks), rows, weight.shape[1]), jnp.bfloat16),
        compiler_params=grant(12),
        name="project",
    )(here, *blocks, weight)


def norm_body(parts_ref, stream_ref, gain_ref, routes_ref, codes_ref, residual_ref, payload_ref):
    seqs, heads, rows, width = parts_ref.shape
    wide = seqs * width
    total = jnp.zeros((rows, 1), jnp.float32)
    for s in range(seqs):
        at = slice(s * width, (s + 1) * width)
        attn = parts_ref[s, 0].astype(jnp.float32)
        for h in range(1, heads):
            attn = attn + parts_ref[s, h].astype(jnp.float32)
        residual = (stream_ref[:, at].astype(jnp.float32) + attn).astype(jnp.bfloat16)
        residual_ref[:, at] = residual
        widened = residual.astype(jnp.float32)
        total = total + jnp.sum(widened * widened, axis=-1, keepdims=True)
    factor = lax.rsqrt(total / wide + epsilon)
    for s in range(seqs):
        at = slice(s * width, (s + 1) * width)
        widened = residual_ref[:, at].astype(jnp.float32)
        normed = (widened * factor * gain_ref[:, at]).astype(jnp.bfloat16)
        payload_ref[:, at] = normed
    top = routes_ref.shape[0]
    tail = jnp.concatenate(
        [
            routes_ref[...].astype(jnp.float32),
            codes_ref[...].astype(jnp.float32),
            jnp.zeros((LANES - 2 * top, rows), jnp.float32),
        ],
        axis=0,
    )
    payload_ref[:, wide:] = tail.T.astype(jnp.bfloat16)


def norm(parts, stream, gain, routes, codes):
    rows, wide = stream.shape
    return pl.pallas_call(
        norm_body,
        out_shape=[
            jax.ShapeDtypeStruct((rows, wide), jnp.bfloat16),
            jax.ShapeDtypeStruct((rows, wide + LANES), jnp.bfloat16),
        ],
        compiler_params=grant(8),
        name="norm",
    )(parts, stream, gain, routes, codes)


def placement(tail, zh, blocks, top, experts_shape, capacity):
    seqs, zs, ys = experts_shape
    tokens = tail.shape[0]
    rows = tokens // blocks
    experts = seqs * ys
    slots = experts * blocks * capacity
    column = iota((tokens, experts), 1)
    name = (div(column, ys) * zs + zh) * ys + rem(column, ys)
    name = name.astype(jnp.float32)
    match = jnp.zeros((tokens, experts), jnp.float32)
    code = jnp.zeros((tokens, experts), jnp.float32)
    for k in range(top):
        hit = tail[:, k : k + 1] == name
        match = jnp.where(hit, 1.0, match)
        code = jnp.where(hit, tail[:, top + k : top + k + 1], code)
    row, col = iota((tokens, tokens), 0), iota((tokens, tokens), 1)
    before = jnp.where((div(row, rows) == div(col, rows)) & (col < row), 1.0, 0.0)
    rank = jnp.dot(
        before.astype(jnp.bfloat16), match.astype(jnp.bfloat16), preferred_element_type=jnp.float32
    )
    rank = jnp.where(match > 0.0, rank, 99.0)
    spread = jnp.where(
        div(iota((experts, slots), 1), blocks * capacity) == iota((experts, slots), 0), 1.0, 0.0
    ).astype(jnp.bfloat16)
    rank = jnp.dot(rank.astype(jnp.bfloat16), spread, preferred_element_type=jnp.float32)
    code = jnp.dot(code.astype(jnp.bfloat16), spread, preferred_element_type=jnp.float32)
    slot = rem(iota((tokens, slots), 1), blocks * capacity)
    at = div(iota((tokens, slots), 0), rows) * capacity + rank.astype(jnp.int32)
    return jnp.where((slot == at) & (rank < capacity), code, 0.0)


def dispatch_body(here_ref, *refs, static):
    *payload_refs, out_ref, code_ref, total_ref = refs
    planes = len(payload_refs)
    wide = out_ref.shape[1]
    top = static["top"]
    tail = jnp.concatenate([r[:, wide:].astype(jnp.float32) for r in payload_refs], axis=0)
    code = placement(tail, here_ref[1], planes, **static)
    place = jnp.where(code > 0.0, 1.0, 0.0).T.astype(jnp.bfloat16)
    tokens = jnp.concatenate([r[:, :wide] for r in payload_refs], axis=0)
    out_ref[...] = jnp.dot(place, tokens, preferred_element_type=jnp.float32).astype(jnp.bfloat16)
    code_ref[...] = code.astype(jnp.bfloat16)
    lane = iota(tail.shape, 1)
    listed = jnp.where((lane >= top) & (lane < 2 * top), tail, 0.0)
    total_ref[...] = jnp.broadcast_to(jnp.sum(listed, axis=-1, keepdims=True), tail.shape)


def dispatch(here, payloads, static):
    seqs, _, ys = static["experts_shape"]
    planes, rows, wide = len(payloads), payloads[0].shape[0], payloads[0].shape[1] - LANES
    tokens, slots = planes * rows, seqs * ys * planes * static["capacity"]
    out, code, total = pl.pallas_call(
        lambda *refs: dispatch_body(*refs, static=static),
        in_specs=[pl.BlockSpec(memory_space=pltpu.SMEM)]
        + [pl.BlockSpec(memory_space=pltpu.VMEM)] * planes,
        out_shape=[
            jax.ShapeDtypeStruct((slots, wide), jnp.bfloat16),
            jax.ShapeDtypeStruct((tokens, slots), jnp.bfloat16),
            jax.ShapeDtypeStruct((tokens, LANES), jnp.float32),
        ],
        compiler_params=grant(16),
        name="dispatch",
    )(here, *payloads)
    return out.reshape(seqs * ys, -1, wide), (code, total)


def expert_body(rows_ref, gate_ref, up_ref, down_hbm, out_ref, down_ref, sem):
    fetch = pltpu.make_async_copy(down_hbm.at[0], down_ref, sem)
    fetch.start()
    rows = rows_ref[...]
    gate = jnp.dot(rows, gate_ref[0], preferred_element_type=jnp.float32)
    up = jnp.dot(rows, up_ref[0], preferred_element_type=jnp.float32)
    act = (gate / (1.0 + jnp.exp(-gate)) * up).astype(jnp.bfloat16)
    fetch.wait()
    part = jnp.dot(act, down_ref[...], preferred_element_type=jnp.float32)
    out_ref[...] = part.astype(jnp.bfloat16)


def expert(arrived, gate_weight, up_weight, down_weight):
    shape = arrived.shape
    wide = shape[-1]
    rows = shape[0] * shape[1]
    return pl.pallas_call(
        expert_body,
        in_specs=[pl.BlockSpec(memory_space=pltpu.VMEM)] * 3 + [pl.BlockSpec(memory_space=pl.ANY)],
        out_shape=jax.ShapeDtypeStruct((rows, wide), jnp.bfloat16),
        scratch_shapes=[
            pltpu.VMEM(down_weight.shape[1:], jnp.bfloat16),
            pltpu.SemaphoreType.DMA,
        ],
        compiler_params=grant(24),
        name="expert",
    )(
        arrived.reshape(rows, wide),
        pltpu.with_memory_space_constraint(gate_weight, pltpu.VMEM),
        pltpu.with_memory_space_constraint(up_weight, pltpu.VMEM),
        *in_hbm(down_weight),
    ).reshape(shape)


def combine_body(code_ref, total_ref, returned_ref, *outs):
    part = jnp.dot(code_ref[...], returned_ref[...], preferred_element_type=jnp.float32)
    part = (part / total_ref[:, :1]).astype(jnp.bfloat16)
    rows = part.shape[0] // len(outs)
    for b, out_ref in enumerate(outs):
        out_ref[...] = part[b * rows : (b + 1) * rows]


def combine(code, total, returned, planes):
    wide = returned.shape[-1]
    rows = code.shape[0] // planes
    return pl.pallas_call(
        combine_body,
        out_shape=[jax.ShapeDtypeStruct((rows, wide), jnp.bfloat16)] * planes,
        compiler_params=grant(10),
        name="combine",
    )(code, total, returned.reshape(-1, wide))


def finish_body(residual_ref, *refs):
    *sum_refs, out_ref = refs
    part = residual_ref[...].astype(jnp.float32)
    for ref in sum_refs:
        part = part + ref[...].astype(jnp.float32)
    out_ref[...] = part.astype(jnp.bfloat16)


def finish(residual, *sums):
    return pl.pallas_call(
        finish_body,
        out_shape=jax.ShapeDtypeStruct(residual.shape, jnp.bfloat16),
        compiler_params=grant(8),
        name="finish",
    )(residual, *sums)


def shift(size, by):
    return [(i, (i + by) % size) for i in range(size)]


def z_moves(lows, highs):
    size = lows * highs

    def index(z):
        return z % size % lows * highs + z % size // lows

    return [
        [(index(z), index(z + (far if z % lows == 0 else -far))) for z in range(size)]
        for far in (2, -1, -3)
    ]


def exchange(blocks, axes):
    return lax.all_to_all(blocks, axes, split_axis=0, concat_axis=0, tiled=True)


def on_device(
    stream,
    queries,
    cache_pairs,
    fresh_pairs,
    kept_slots,
    segment_kept_count,
    output_weight,
    norm_gain,
    routes,
    gate_codes,
    gate_weight,
    up_weight,
    down_weight,
):
    rows, wide = stream.shape
    seqs, zs, ys = (lax.axis_size(a) for a in ("seq", "zh", "y"))
    here = jnp.stack([lax.axis_index("seq"), lax.axis_index("zh")]).astype(jnp.int32)
    experts = seqs * zs * ys
    static = dict(
        top=routes.shape[1],
        experts_shape=(seqs, zs, ys),
        capacity=min(rows, max(2, 2 * rows * routes.shape[1] // experts)),
    )

    head_out = attention(
        kept_slots[:, 0].T, segment_kept_count[:, 0].T, queries, cache_pairs, fresh_pairs[:, 0]
    )
    head_blocks = [head_out] + [
        lax.ppermute(head_out, "seq", shift(seqs, d)) for d in STEPS[1:]
    ]
    parts = project(here, head_blocks, output_weight)
    parts = exchange(parts.reshape(-1, rows, parts.shape[-1]), ("seq",) + HEADS)
    parts = parts.reshape(seqs, -1, rows, parts.shape[-1])
    residual, payload = norm(
        parts, stream, norm_gain.reshape(1, -1), routes.T, gate_codes.T
    )
    moves = z_moves(lax.axis_size("zl"), zs)
    payloads = [payload] + [lax.ppermute(payload, ("zl", "zh"), m) for m in moves]
    sent, mix = dispatch(here, payloads, static)
    made = expert(exchange(sent, PLANE), gate_weight, up_weight, down_weight)
    own, *sums = combine(*mix, exchange(made, PLANE), len(payloads))
    back = [[(b, a) for a, b in m] for m in moves]
    sums = [lax.ppermute(v, ("zl", "zh"), m) for v, m in zip(sums, back)]
    return finish(residual, own, *sums)


def solution(mesh):
    fine = Mesh(mesh.devices.reshape(2, 2, mesh.shape["seq"], 4, 4), MESH_AXES)
    heads, req = HEADS, ("zh", "y")
    tokens = P(req + ("seq",) + heads, None)
    requests = req + ("seq",)
    owned = P(("seq",) + req, None, None)
    placed = (
        tokens,
        P(requests, heads),
        P(requests, heads, None, None),
        P(requests, heads, None),
        P(requests, heads, None),
        P(requests, heads, None),
        P(heads, "seq"),
        P(),
        tokens,
        tokens,
        owned,
        owned,
        owned,
    )
    return jax.shard_map(
        on_device, mesh=fine, in_specs=placed, out_specs=tokens, check_vma=False
    )
```

```python
import jax
import jax.numpy as jnp
from jax import lax
from jax.experimental import pallas as pl
from jax.experimental.pallas import tpu as pltpu
from jax.sharding import Mesh
from jax.sharding import PartitionSpec as P

epsilon = 1e-06
LANES = 128
OFFSET_NS = 14000
ATT_BLOCK = 32
MESH_AXES = ("zl", "core", "seq", "zh", "y")
PLANE = ("seq", "y")
HEADS = ("zl", "core")
STEPS = (0, 1, 3, 2)


def grant(mib):
    return pltpu.CompilerParams(vmem_limit_bytes=mib * 2**20)


def in_hbm(*arrays):
    return [pltpu.with_memory_space_constraint(a, pltpu.HBM) for a in arrays]


def iota(shape, dim):
    return lax.broadcasted_iota(jnp.int32, shape, dim)


def div(a, b):
    return lax.div(a, jnp.full_like(a, b))


def rem(a, b):
    return lax.rem(a, jnp.full_like(a, b))


def attention_body(slots_ref, counts_ref, query_ref, cache_ref, fresh_ref, out_ref, bias_ref):
    rows, _, positions, pair = cache_ref.shape
    head_dim = pair // 2
    group = query_ref.shape[1] // head_dim
    scale = head_dim ** (-0.5)
    step = pl.program_id(0)

    @pl.when(step == 0)
    def _():
        listed, all_rows = slots_ref.shape
        segments = counts_ref.shape[0]
        keep = listed // segments
        seg_length = positions // segments
        counts = counts_ref[...].astype(jnp.float32)
        limit = jnp.concatenate(
            [jnp.broadcast_to(counts[s : s + 1], (keep, all_rows)) for s in range(segments)], axis=0
        )
        rank = rem(iota((listed, all_rows), 0), keep).astype(jnp.float32)
        valid = jnp.where(rank < limit, slots_ref[...].astype(jnp.float32), 99.0)
        valid = valid.astype(jnp.bfloat16)
        place = rem(iota((positions, all_rows), 0), seg_length).astype(jnp.float32)
        source = iota((positions, listed), 1)
        wanted = div(iota((positions, listed), 0), seg_length) * keep
        bias = jnp.full((positions, all_rows), -1e30, jnp.float32)
        for j in range(keep):
            pick = jnp.where(source == wanted + j, 1.0, 0.0).astype(jnp.bfloat16)
            here = jnp.dot(pick, valid, preferred_element_type=jnp.float32)
            bias = jnp.where(here == place, 0.0, bias)
        bias_ref[...] = bias.T

    query = query_ref[...].reshape(rows, group, head_dim)
    keys = cache_ref[:, 0, :, :head_dim]
    values = cache_ref[:, 0, :, head_dim:]
    fresh = fresh_ref[...].astype(jnp.float32)
    scores = jnp.einsum("rgd,rpd->rgp", query, keys, preferred_element_type=jnp.float32) * scale
    bias = bias_ref[pl.ds(pl.multiple_of(step * rows, rows), rows), :]
    scores = scores + bias[:, None, :]
    own = jnp.sum(
        query.astype(jnp.float32) * fresh[:, None, :head_dim], axis=-1, keepdims=True
    ) * scale
    top = jnp.maximum(jnp.max(scores, axis=-1, keepdims=True), own)
    probs = jnp.exp(scores - top).astype(jnp.bfloat16)
    take_new = jnp.exp(own - top)
    denom = jnp.sum(probs.astype(jnp.float32), axis=-1, keepdims=True) + take_new
    numer = jnp.einsum("rgp,rpd->rgd", probs, values, preferred_element_type=jnp.float32)
    numer = numer + take_new * fresh[:, None, head_dim:]
    out_ref[...] = (numer / denom).astype(jnp.bfloat16).reshape(rows, group * head_dim)


def attention(slots, counts, queries, cache_pairs, fresh):
    rows, width = queries.shape
    block = min(ATT_BLOCK, rows)
    return pl.pallas_call(
        attention_body,
        grid=(rows // block,),
        in_specs=[
            pl.BlockSpec(slots.shape, lambda i: (0, 0)),
            pl.BlockSpec(counts.shape, lambda i: (0, 0)),
            pl.BlockSpec((block, width), lambda i: (i, 0)),
            pl.BlockSpec((block,) + cache_pairs.shape[1:], lambda i: (i, 0, 0, 0)),
            pl.BlockSpec((block, fresh.shape[1]), lambda i: (i, 0)),
        ],
        out_specs=pl.BlockSpec((block, width), lambda i: (i, 0)),
        out_shape=jax.ShapeDtypeStruct((rows, width), jnp.bfloat16),
        scratch_shapes=[pltpu.VMEM((rows, cache_pairs.shape[2]), jnp.float32)],
        compiler_params=grant(24),
        name="attention",
    )(*in_hbm(slots, counts, queries, cache_pairs, fresh))


def project_body(here_ref, *refs):
    *head_refs, weight_ref, out_ref = refs
    count = len(head_refs)
    weight = weight_ref[...]
    for step, head_ref in zip(STEPS, head_refs):
        part = jnp.dot(head_ref[...], weight, preferred_element_type=jnp.float32)
        out_ref[(here_ref[0] + (count - step)) & (count - 1)] = part.astype(jnp.bfloat16)


def project(here, blocks, weight):
    rows = blocks[0].shape[0]
    return pl.pallas_call(
        project_body,
        in_specs=[pl.BlockSpec(memory_space=pltpu.SMEM)]
        + [pl.BlockSpec(memory_space=pltpu.VMEM)] * (len(blocks) + 1),
        out_shape=jax.ShapeDtypeStruct((len(blocks), rows, weight.shape[1]), jnp.bfloat16),
        compiler_params=grant(12),
        name="project",
    )(here, *blocks, weight)


def norm_body(here_ref, parts_ref, stream_ref, gain_ref, routes_ref, codes_ref, residual_ref, payload_ref):
    seqs, heads, rows, width = parts_ref.shape
    wide = seqs * width
    total = jnp.zeros((rows, 1), jnp.float32)
    for s in range(seqs):
        at = slice(s * width, (s + 1) * width)
        attn = parts_ref[s, 0].astype(jnp.float32)
        for h in range(1, heads):
            attn = attn + parts_ref[s, h].astype(jnp.float32)
        residual = (stream_ref[:, at].astype(jnp.float32) + attn).astype(jnp.bfloat16)
        residual_ref[:, at] = residual
        widened = residual.astype(jnp.float32)
        total = total + jnp.sum(widened * widened, axis=-1, keepdims=True)
    factor = lax.rsqrt(total / wide + epsilon)
    for s in range(seqs):
        at = slice(s * width, (s + 1) * width)
        widened = residual_ref[:, at].astype(jnp.float32)
        normed = (widened * factor * gain_ref[:, at]).astype(jnp.bfloat16)
        payload_ref[:, at] = normed
    top = routes_ref.shape[0]
    tail = jnp.concatenate(
        [
            routes_ref[...].astype(jnp.float32),
            codes_ref[...].astype(jnp.float32),
            jnp.zeros((LANES - 2 * top, rows), jnp.float32),
        ],
        axis=0,
    )
    payload_ref[:, wide:] = tail.T.astype(jnp.bfloat16)

    @pl.when(here_ref[2] == 1)
    def _():
        pl.delay(OFFSET_NS)


def norm(here, parts, stream, gain, routes, codes):
    rows, wide = stream.shape
    return pl.pallas_call(
        norm_body,
        in_specs=[pl.BlockSpec(memory_space=pltpu.SMEM)]
        + [pl.BlockSpec(memory_space=pltpu.VMEM)] * 5,
        out_shape=[
            jax.ShapeDtypeStruct((rows, wide), jnp.bfloat16),
            jax.ShapeDtypeStruct((rows, wide + LANES), jnp.bfloat16),
        ],
        compiler_params=grant(8),
        name="norm",
    )(here, parts, stream, gain, routes, codes)


def placement(tail, zh, blocks, top, experts_shape, capacity):
    seqs, zs, ys = experts_shape
    tokens = tail.shape[0]
    rows = tokens // blocks
    experts = seqs * ys
    slots = experts * blocks * capacity
    column = iota((tokens, experts), 1)
    name = (div(column, ys) * zs + zh) * ys + rem(column, ys)
    name = name.astype(jnp.float32)
    match = jnp.zeros((tokens, experts), jnp.float32)
    code = jnp.zeros((tokens, experts), jnp.float32)
    for k in range(top):
        hit = tail[:, k : k + 1] == name
        match = jnp.where(hit, 1.0, match)
        code = jnp.where(hit, tail[:, top + k : top + k + 1], code)
    row, col = iota((tokens, tokens), 0), iota((tokens, tokens), 1)
    before = jnp.where((div(row, rows) == div(col, rows)) & (col < row), 1.0, 0.0)
    rank = jnp.dot(
        before.astype(jnp.bfloat16), match.astype(jnp.bfloat16), preferred_element_type=jnp.float32
    )
    rank = jnp.where(match > 0.0, rank, 99.0)
    spread = jnp.where(
        div(iota((experts, slots), 1), blocks * capacity) == iota((experts, slots), 0), 1.0, 0.0
    ).astype(jnp.bfloat16)
    rank = jnp.dot(rank.astype(jnp.bfloat16), spread, preferred_element_type=jnp.float32)
    code = jnp.dot(code.astype(jnp.bfloat16), spread, preferred_element_type=jnp.float32)
    slot = rem(iota((tokens, slots), 1), blocks * capacity)
    at = div(iota((tokens, slots), 0), rows) * capacity + rank.astype(jnp.int32)
    return jnp.where((slot == at) & (rank < capacity), code, 0.0)


def dispatch_body(here_ref, *refs, static):
    *payload_refs, out_ref, code_ref, total_ref = refs
    planes = len(payload_refs)
    wide = out_ref.shape[1]
    top = static["top"]
    tail = jnp.concatenate([r[:, wide:].astype(jnp.float32) for r in payload_refs], axis=0)
    code = placement(tail, here_ref[1], planes, **static)
    place = jnp.where(code > 0.0, 1.0, 0.0).T.astype(jnp.bfloat16)
    tokens = jnp.concatenate([r[:, :wide] for r in payload_refs], axis=0)
    out_ref[...] = jnp.dot(place, tokens, preferred_element_type=jnp.float32).astype(jnp.bfloat16)
    code_ref[...] = code.astype(jnp.bfloat16)
    lane = iota(tail.shape, 1)
    listed = jnp.where((lane >= top) & (lane < 2 * top), tail, 0.0)
    total_ref[...] = jnp.broadcast_to(jnp.sum(listed, axis=-1, keepdims=True), tail.shape)


def dispatch(here, payloads, static):
    seqs, _, ys = static["experts_shape"]
    planes, rows, wide = len(payloads), payloads[0].shape[0], payloads[0].shape[1] - LANES
    tokens, slots = planes * rows, seqs * ys * planes * static["capacity"]
    out, code, total = pl.pallas_call(
        lambda *refs: dispatch_body(*refs, static=static),
        in_specs=[pl.BlockSpec(memory_space=pltpu.SMEM)]
        + [pl.BlockSpec(memory_space=pltpu.VMEM)] * planes,
        out_shape=[
            jax.ShapeDtypeStruct((slots, wide), jnp.bfloat16),
            jax.ShapeDtypeStruct((tokens, slots), jnp.bfloat16),
            jax.ShapeDtypeStruct((tokens, LANES), jnp.float32),
        ],
        compiler_params=grant(16),
        name="dispatch",
    )(here, *payloads)
    return out.reshape(seqs * ys, -1, wide), (code, total)


def expert_body(rows_ref, gate_ref, up_ref, down_hbm, out_ref, down_ref, sem):
    fetch = pltpu.make_async_copy(down_hbm.at[0], down_ref, sem)
    fetch.start()
    rows = rows_ref[...]
    gate = jnp.dot(rows, gate_ref[0], preferred_element_type=jnp.float32)
    up = jnp.dot(rows, up_ref[0], preferred_element_type=jnp.float32)
    act = (gate / (1.0 + jnp.exp(-gate)) * up).astype(jnp.bfloat16)
    fetch.wait()
    part = jnp.dot(act, down_ref[...], preferred_element_type=jnp.float32)
    out_ref[...] = part.astype(jnp.bfloat16)


def expert(arrived, gate_weight, up_weight, down_weight):
    shape = arrived.shape
    wide = shape[-1]
    rows = shape[0] * shape[1]
    return pl.pallas_call(
        expert_body,
        in_specs=[pl.BlockSpec(memory_space=pltpu.VMEM)] * 3 + [pl.BlockSpec(memory_space=pl.ANY)],
        out_shape=jax.ShapeDtypeStruct((rows, wide), jnp.bfloat16),
        scratch_shapes=[
            pltpu.VMEM(down_weight.shape[1:], jnp.bfloat16),
            pltpu.SemaphoreType.DMA,
        ],
        compiler_params=grant(24),
        name="expert",
    )(
        arrived.reshape(rows, wide),
        pltpu.with_memory_space_constraint(gate_weight, pltpu.VMEM),
        pltpu.with_memory_space_constraint(up_weight, pltpu.VMEM),
        *in_hbm(down_weight),
    ).reshape(shape)


def combine_body(code_ref, total_ref, returned_ref, *outs):
    part = jnp.dot(code_ref[...], returned_ref[...], preferred_element_type=jnp.float32)
    part = (part / total_ref[:, :1]).astype(jnp.bfloat16)
    rows = part.shape[0] // len(outs)
    for b, out_ref in enumerate(outs):
        out_ref[...] = part[b * rows : (b + 1) * rows]


def combine(code, total, returned, planes):
    wide = returned.shape[-1]
    rows = code.shape[0] // planes
    return pl.pallas_call(
        combine_body,
        out_shape=[jax.ShapeDtypeStruct((rows, wide), jnp.bfloat16)] * planes,
        compiler_params=grant(10),
        name="combine",
    )(code, total, returned.reshape(-1, wide))


def finish_body(residual_ref, *refs):
    *sum_refs, out_ref = refs
    part = residual_ref[...].astype(jnp.float32)
    for ref in sum_refs:
        part = part + ref[...].astype(jnp.float32)
    out_ref[...] = part.astype(jnp.bfloat16)


def finish(residual, *sums):
    return pl.pallas_call(
        finish_body,
        out_shape=jax.ShapeDtypeStruct(residual.shape, jnp.bfloat16),
        compiler_params=grant(8),
        name="finish",
    )(residual, *sums)


def shift(size, by):
    return [(i, (i + by) % size) for i in range(size)]


def z_moves(lows, highs):
    size = lows * highs

    def index(z):
        return z % size % lows * highs + z % size // lows

    return [
        [(index(z), index(z + (far if z % lows == 0 else -far))) for z in range(size)]
        for far in (2, -1, -3)
    ]


def exchange(blocks, axes):
    return lax.all_to_all(blocks, axes, split_axis=0, concat_axis=0, tiled=True)


def on_device(
    stream,
    queries,
    cache_pairs,
    fresh_pairs,
    kept_slots,
    segment_kept_count,
    output_weight,
    norm_gain,
    routes,
    gate_codes,
    gate_weight,
    up_weight,
    down_weight,
):
    rows, wide = stream.shape
    seqs, zs, ys = (lax.axis_size(a) for a in ("seq", "zh", "y"))
    here = jnp.stack([lax.axis_index(a) for a in ("seq", "zh", "core")]).astype(jnp.int32)
    experts = seqs * zs * ys
    static = dict(
        top=routes.shape[1],
        experts_shape=(seqs, zs, ys),
        capacity=min(rows, max(2, 2 * rows * routes.shape[1] // experts)),
    )

    head_out = attention(
        kept_slots[:, 0].T, segment_kept_count[:, 0].T, queries, cache_pairs, fresh_pairs[:, 0]
    )
    head_blocks = [head_out] + [
        lax.ppermute(head_out, "seq", shift(seqs, d)) for d in STEPS[1:]
    ]
    parts = project(here, head_blocks, output_weight)
    parts = exchange(parts.reshape(-1, rows, parts.shape[-1]), ("seq",) + HEADS)
    parts = parts.reshape(seqs, -1, rows, parts.shape[-1])
    residual, payload = norm(
        here, parts, stream, norm_gain.reshape(1, -1), routes.T, gate_codes.T
    )
    moves = z_moves(lax.axis_size("zl"), zs)
    payloads = [payload] + [lax.ppermute(payload, ("zl", "zh"), m) for m in moves]
    sent, mix = dispatch(here, payloads, static)
    made = expert(exchange(sent, PLANE), gate_weight, up_weight, down_weight)
    own, *sums = combine(*mix, exchange(made, PLANE), len(payloads))
    back = [[(b, a) for a, b in m] for m in moves]
    sums = [lax.ppermute(v, ("zl", "zh"), m) for v, m in zip(sums, back)]
    return finish(residual, own, *sums)


def solution(mesh):
    fine = Mesh(mesh.devices.reshape(2, 2, mesh.shape["seq"], 4, 4), MESH_AXES)
    heads, req = HEADS, ("zh", "y")
    tokens = P(req + ("seq",) + heads, None)
    requests = req + ("seq",)
    owned = P(("seq",) + req, None, None)
    placed = (
        tokens,
        P(requests, heads),
        P(requests, heads, None, None),
        P(requests, heads, None),
        P(requests, heads, None),
        P(requests, heads, None),
        P(heads, "seq"),
        P(),
        tokens,
        tokens,
        owned,
        owned,
        owned,
    )
    return jax.shard_map(
        on_device, mesh=fine, in_specs=placed, out_specs=tokens, check_vma=False
    )
```

```python
import functools

import jax
import jax.numpy as jnp
from jax import lax
from jax.experimental import pallas as pl
from jax.experimental.pallas import tpu as pltpu
from jax.sharding import Mesh
from jax.sharding import PartitionSpec as P

epsilon = 1e-06
LANES = 128
OFFSET_NS = 14000
ATT_BLOCK = 32
ATT_PARTS = 2
MESH_AXES = ("zl", "core", "seq", "zh", "y")
PLANE = ("seq", "y")
HEADS = ("zl", "core")
STEPS = (0, 1, 3, 2)


def grant(mib):
    return pltpu.CompilerParams(vmem_limit_bytes=mib * 2**20)


def in_hbm(*arrays):
    return [pltpu.with_memory_space_constraint(a, pltpu.HBM) for a in arrays]


def iota(shape, dim):
    return lax.broadcasted_iota(jnp.int32, shape, dim)


def div(a, b):
    return lax.div(a, jnp.full_like(a, b))


def rem(a, b):
    return lax.rem(a, jnp.full_like(a, b))


def attention_body(slots_ref, counts_ref, query_ref, cache_ref, fresh_ref, out_ref, bias_ref, *, first):
    rows, _, positions, pair = cache_ref.shape
    head_dim = pair // 2
    group = query_ref.shape[1] // head_dim
    scale = head_dim ** (-0.5)
    step = pl.program_id(0)

    @pl.when(step == 0)
    def _():
        listed, all_rows = slots_ref.shape
        segments = counts_ref.shape[0]
        keep = listed // segments
        seg_length = positions // segments
        counts = counts_ref[...].astype(jnp.float32)
        limit = jnp.concatenate(
            [jnp.broadcast_to(counts[s : s + 1], (keep, all_rows)) for s in range(segments)], axis=0
        )
        rank = rem(iota((listed, all_rows), 0), keep).astype(jnp.float32)
        valid = jnp.where(rank < limit, slots_ref[...].astype(jnp.float32), 99.0)
        valid = valid.astype(jnp.bfloat16)
        place = rem(iota((positions, all_rows), 0), seg_length).astype(jnp.float32)
        source = iota((positions, listed), 1)
        wanted = div(iota((positions, listed), 0), seg_length) * keep
        bias = jnp.full((positions, all_rows), -1e30, jnp.float32)
        for j in range(keep):
            pick = jnp.where(source == wanted + j, 1.0, 0.0).astype(jnp.bfloat16)
            here = jnp.dot(pick, valid, preferred_element_type=jnp.float32)
            bias = jnp.where(here == place, 0.0, bias)
        bias_ref[...] = bias.T

    query = query_ref[...].reshape(rows, group, head_dim)
    keys = cache_ref[:, 0, :, :head_dim]
    values = cache_ref[:, 0, :, head_dim:]
    fresh = fresh_ref[...].astype(jnp.float32)
    both = jnp.einsum(
        "rgd,rpd->rgp",
        query.reshape(rows // 2, 2 * group, head_dim),
        keys.reshape(rows // 2, 2 * positions, head_dim),
        preferred_element_type=jnp.float32,
    )
    scores = jnp.stack([both[:, :group, :positions], both[:, group:, positions:]], axis=1)
    scores = scores.reshape(rows, group, positions) * scale
    bias = bias_ref[pl.ds(pl.multiple_of((first + step) * rows, rows), rows), :]
    scores = scores + bias[:, None, :]
    own = jnp.sum(
        query.astype(jnp.float32) * fresh[:, None, :head_dim], axis=-1, keepdims=True
    ) * scale
    top = jnp.maximum(jnp.max(scores, axis=-1, keepdims=True), own)
    probs = jnp.exp(scores - top).astype(jnp.bfloat16)
    take_new = jnp.exp(own - top)
    denom = jnp.sum(probs.astype(jnp.float32), axis=-1, keepdims=True) + take_new
    numer = jnp.einsum("rgp,rpd->rgd", probs, values, preferred_element_type=jnp.float32)
    numer = numer + take_new * fresh[:, None, head_dim:]
    out_ref[...] = (numer / denom).astype(jnp.bfloat16).reshape(rows, group * head_dim)


def attention(slots, counts, queries, cache_pairs, fresh, part, parts):
    rows, width = queries.shape
    block = min(ATT_BLOCK, rows // parts)
    steps = rows // parts // block
    first = part * steps
    return pl.pallas_call(
        functools.partial(attention_body, first=first),
        grid=(steps,),
        in_specs=[
            pl.BlockSpec(slots.shape, lambda i: (0, 0)),
            pl.BlockSpec(counts.shape, lambda i: (0, 0)),
            pl.BlockSpec((block, width), lambda i: (first + i, 0)),
            pl.BlockSpec((block,) + cache_pairs.shape[1:], lambda i: (first + i, 0, 0, 0)),
            pl.BlockSpec((block, fresh.shape[1]), lambda i: (first + i, 0)),
        ],
        out_specs=pl.BlockSpec((block, width), lambda i: (i, 0)),
        out_shape=jax.ShapeDtypeStruct((rows // parts, width), jnp.bfloat16),
        scratch_shapes=[pltpu.VMEM((rows, cache_pairs.shape[2]), jnp.float32)],
        compiler_params=grant(24),
        name="attention",
    )(*in_hbm(slots, counts, queries, cache_pairs, fresh))


def project_body(here_ref, *refs):
    *head_refs, weight_ref, out_ref = refs
    earlier_ref = None
    if len(head_refs) > len(STEPS):
        earlier_ref, *head_refs = head_refs
    count, half = len(STEPS), head_refs[0].shape[0]
    heads = jnp.concatenate([r[...] for r in head_refs], axis=0)
    made = jnp.dot(heads, weight_ref[...], preferred_element_type=jnp.float32)
    made = made.astype(jnp.bfloat16)
    start = 0
    if earlier_ref is not None:
        start = earlier_ref.shape[1]
        out_ref[:, :start] = earlier_ref[...]
    for n, step in enumerate(STEPS):
        at = (here_ref[0] + (count - step)) & (count - 1)
        out_ref[at, start : start + half] = made[n * half : (n + 1) * half]


def project(here, earlier, blocks, weight):
    rows = blocks[0].shape[0] + sum(e.shape[1] for e in earlier)
    operands = [*earlier, *blocks, weight]
    return pl.pallas_call(
        project_body,
        in_specs=[pl.BlockSpec(memory_space=pltpu.SMEM)]
        + [pl.BlockSpec(memory_space=pltpu.VMEM)] * len(operands),
        out_shape=jax.ShapeDtypeStruct((len(blocks), rows, weight.shape[1]), jnp.bfloat16),
        compiler_params=grant(12),
        name="project",
    )(here, *operands)


def norm_body(here_ref, parts_ref, stream_ref, gain_ref, routes_ref, codes_ref, residual_ref, payload_ref):
    seqs, heads, rows, width = parts_ref.shape
    wide = seqs * width
    total = jnp.zeros((rows, 1), jnp.float32)
    for s in range(seqs):
        at = slice(s * width, (s + 1) * width)
        attn = parts_ref[s, 0].astype(jnp.float32)
        for h in range(1, heads):
            attn = attn + parts_ref[s, h].astype(jnp.float32)
        residual = (stream_ref[:, at].astype(jnp.float32) + attn).astype(jnp.bfloat16)
        residual_ref[:, at] = residual
        widened = residual.astype(jnp.float32)
        total = total + jnp.sum(widened * widened, axis=-1, keepdims=True)
    factor = lax.rsqrt(total / wide + epsilon)
    for s in range(seqs):
        at = slice(s * width, (s + 1) * width)
        widened = residual_ref[:, at].astype(jnp.float32)
        normed = (widened * factor * gain_ref[:, at]).astype(jnp.bfloat16)
        payload_ref[:, at] = normed
    top = routes_ref.shape[0]
    tail = jnp.concatenate(
        [
            routes_ref[...].astype(jnp.float32),
            codes_ref[...].astype(jnp.float32),
            jnp.zeros((LANES - 2 * top, rows), jnp.float32),
        ],
        axis=0,
    )
    payload_ref[:, wide:] = tail.T.astype(jnp.bfloat16)

    @pl.when(here_ref[2] == 1)
    def _():
        pl.delay(OFFSET_NS)


def norm(here, parts, stream, gain, routes, codes):
    rows, wide = stream.shape
    return pl.pallas_call(
        norm_body,
        in_specs=[pl.BlockSpec(memory_space=pltpu.SMEM)]
        + [pl.BlockSpec(memory_space=pltpu.VMEM)] * 5,
        out_shape=[
            jax.ShapeDtypeStruct((rows, wide), jnp.bfloat16),
            jax.ShapeDtypeStruct((rows, wide + LANES), jnp.bfloat16),
        ],
        compiler_params=grant(8),
        name="norm",
    )(here, parts, stream, gain, routes, codes)


def placement(tail, zh, blocks, top, experts_shape, capacity):
    seqs, zs, ys = experts_shape
    tokens = tail.shape[0]
    rows = tokens // blocks
    experts = seqs * ys
    slots = experts * blocks * capacity
    column = iota((tokens, experts), 1)
    name = (div(column, ys) * zs + zh) * ys + rem(column, ys)
    name = name.astype(jnp.float32)
    match = jnp.zeros((tokens, experts), jnp.float32)
    code = jnp.zeros((tokens, experts), jnp.float32)
    for k in range(top):
        hit = tail[:, k : k + 1] == name
        match = jnp.where(hit, 1.0, match)
        code = jnp.where(hit, tail[:, top + k : top + k + 1], code)
    row, col = iota((tokens, tokens), 0), iota((tokens, tokens), 1)
    before = jnp.where((div(row, rows) == div(col, rows)) & (col < row), 1.0, 0.0)
    rank = jnp.dot(
        before.astype(jnp.bfloat16), match.astype(jnp.bfloat16), preferred_element_type=jnp.float32
    )
    rank = jnp.where(match > 0.0, rank, 99.0)
    spread = jnp.where(
        div(iota((experts, slots), 1), blocks * capacity) == iota((experts, slots), 0), 1.0, 0.0
    ).astype(jnp.bfloat16)
    rank = jnp.dot(rank.astype(jnp.bfloat16), spread, preferred_element_type=jnp.float32)
    code = jnp.dot(code.astype(jnp.bfloat16), spread, preferred_element_type=jnp.float32)
    slot = rem(iota((tokens, slots), 1), blocks * capacity)
    at = div(iota((tokens, slots), 0), rows) * capacity + rank.astype(jnp.int32)
    return jnp.where((slot == at) & (rank < capacity), code, 0.0)


def dispatch_body(here_ref, *refs, static):
    *payload_refs, out_ref, code_ref, total_ref = refs
    planes = len(payload_refs)
    wide = out_ref.shape[1]
    top = static["top"]
    tail = jnp.concatenate([r[:, wide:].astype(jnp.float32) for r in payload_refs], axis=0)
    code = placement(tail, here_ref[1], planes, **static)
    place = jnp.where(code > 0.0, 1.0, 0.0).T.astype(jnp.bfloat16)
    tokens = jnp.concatenate([r[:, :wide] for r in payload_refs], axis=0)
    out_ref[...] = jnp.dot(place, tokens, preferred_element_type=jnp.float32).astype(jnp.bfloat16)
    code_ref[...] = code.astype(jnp.bfloat16)
    lane = iota(tail.shape, 1)
    listed = jnp.where((lane >= top) & (lane < 2 * top), tail, 0.0)
    total_ref[...] = jnp.broadcast_to(jnp.sum(listed, axis=-1, keepdims=True), tail.shape)


def dispatch(here, payloads, static):
    seqs, _, ys = static["experts_shape"]
    planes, rows, wide = len(payloads), payloads[0].shape[0], payloads[0].shape[1] - LANES
    tokens, slots = planes * rows, seqs * ys * planes * static["capacity"]
    out, code, total = pl.pallas_call(
        lambda *refs: dispatch_body(*refs, static=static),
        in_specs=[pl.BlockSpec(memory_space=pltpu.SMEM)]
        + [pl.BlockSpec(memory_space=pltpu.VMEM)] * planes,
        out_shape=[
            jax.ShapeDtypeStruct((slots, wide), jnp.bfloat16),
            jax.ShapeDtypeStruct((tokens, slots), jnp.bfloat16),
            jax.ShapeDtypeStruct((tokens, LANES), jnp.float32),
        ],
        compiler_params=grant(16),
        name="dispatch",
    )(here, *payloads)
    return out.reshape(seqs * ys, -1, wide), (code, total)


def expert_body(rows_ref, gate_ref, up_ref, down_hbm, out_ref, down_ref, sem):
    fetch = pltpu.make_async_copy(down_hbm.at[0], down_ref, sem)
    fetch.start()
    rows = rows_ref[...]
    gate = jnp.dot(rows, gate_ref[0], preferred_element_type=jnp.float32)
    up = jnp.dot(rows, up_ref[0], preferred_element_type=jnp.float32)
    act = (gate / (1.0 + jnp.exp(-gate)) * up).astype(jnp.bfloat16)
    fetch.wait()
    part = jnp.dot(act, down_ref[...], preferred_element_type=jnp.float32)
    out_ref[...] = part.astype(jnp.bfloat16)


def expert(arrived, gate_weight, up_weight, down_weight):
    shape = arrived.shape
    wide = shape[-1]
    rows = shape[0] * shape[1]
    return pl.pallas_call(
        expert_body,
        in_specs=[pl.BlockSpec(memory_space=pltpu.VMEM)] * 3 + [pl.BlockSpec(memory_space=pl.ANY)],
        out_shape=jax.ShapeDtypeStruct((rows, wide), jnp.bfloat16),
        scratch_shapes=[
            pltpu.VMEM(down_weight.shape[1:], jnp.bfloat16),
            pltpu.SemaphoreType.DMA,
        ],
        compiler_params=grant(24),
        name="expert",
    )(
        arrived.reshape(rows, wide),
        pltpu.with_memory_space_constraint(gate_weight, pltpu.VMEM),
        pltpu.with_memory_space_constraint(up_weight, pltpu.VMEM),
        *in_hbm(down_weight),
    ).reshape(shape)


def combine_body(code_ref, total_ref, returned_ref, *outs):
    part = jnp.dot(code_ref[...], returned_ref[...], preferred_element_type=jnp.float32)
    part = (part / total_ref[:, :1]).astype(jnp.bfloat16)
    rows = part.shape[0] // len(outs)
    for b, out_ref in enumerate(outs):
        out_ref[...] = part[b * rows : (b + 1) * rows]


def combine(code, total, returned, planes):
    wide = returned.shape[-1]
    rows = code.shape[0] // planes
    return pl.pallas_call(
        combine_body,
        out_shape=[jax.ShapeDtypeStruct((rows, wide), jnp.bfloat16)] * planes,
        compiler_params=grant(10),
        name="combine",
    )(code, total, returned.reshape(-1, wide))


def finish_body(residual_ref, *refs):
    *sum_refs, out_ref = refs
    part = residual_ref[...].astype(jnp.float32)
    for ref in sum_refs:
        part = part + ref[...].astype(jnp.float32)
    out_ref[...] = part.astype(jnp.bfloat16)


def finish(residual, *sums):
    return pl.pallas_call(
        finish_body,
        out_shape=jax.ShapeDtypeStruct(residual.shape, jnp.bfloat16),
        compiler_params=grant(8),
        name="finish",
    )(residual, *sums)


def shift(size, by):
    return [(i, (i + by) % size) for i in range(size)]


def z_moves(lows, highs):
    size = lows * highs

    def index(z):
        return z % size % lows * highs + z % size // lows

    return [
        [(index(z), index(z + (far if z % lows == 0 else -far))) for z in range(size)]
        for far in (2, -1, -3)
    ]


def exchange(blocks, axes):
    return lax.all_to_all(blocks, axes, split_axis=0, concat_axis=0, tiled=True)


def on_device(
    stream,
    queries,
    cache_pairs,
    fresh_pairs,
    kept_slots,
    segment_kept_count,
    output_weight,
    norm_gain,
    routes,
    gate_codes,
    gate_weight,
    up_weight,
    down_weight,
):
    rows, wide = stream.shape
    seqs, zs, ys = (lax.axis_size(a) for a in ("seq", "zh", "y"))
    here = jnp.stack([lax.axis_index(a) for a in ("seq", "zh", "core")]).astype(jnp.int32)
    experts = seqs * zs * ys
    static = dict(
        top=routes.shape[1],
        experts_shape=(seqs, zs, ys),
        capacity=min(rows, max(2, 2 * rows * routes.shape[1] // experts)),
    )

    made = []
    for part in range(ATT_PARTS):
        head_out = attention(
            kept_slots[:, 0].T,
            segment_kept_count[:, 0].T,
            queries,
            cache_pairs,
            fresh_pairs[:, 0],
            part,
            ATT_PARTS,
        )
        blocks = [head_out] + [lax.ppermute(head_out, "seq", shift(seqs, d)) for d in STEPS[1:]]
        made = [project(here, made, blocks, output_weight)]
    parts = made[0]
    parts = exchange(parts.reshape(-1, rows, parts.shape[-1]), ("seq",) + HEADS)
    parts = parts.reshape(seqs, -1, rows, parts.shape[-1])
    residual, payload = norm(
        here, parts, stream, norm_gain.reshape(1, -1), routes.T, gate_codes.T
    )
    moves = z_moves(lax.axis_size("zl"), zs)
    payloads = [payload] + [lax.ppermute(payload, ("zl", "zh"), m) for m in moves]
    sent, mix = dispatch(here, payloads, static)
    made = expert(exchange(sent, PLANE), gate_weight, up_weight, down_weight)
    own, *sums = combine(*mix, exchange(made, PLANE), len(payloads))
    back = [[(b, a) for a, b in m] for m in moves]
    sums = [lax.ppermute(v, ("zl", "zh"), m) for v, m in zip(sums, back)]
    return finish(residual, own, *sums)


def solution(mesh):
    fine = Mesh(mesh.devices.reshape(2, 2, mesh.shape["seq"], 4, 4), MESH_AXES)
    heads, req = HEADS, ("zh", "y")
    tokens = P(req + ("seq",) + heads, None)
    requests = req + ("seq",)
    owned = P(("seq",) + req, None, None)
    placed = (
        tokens,
        P(requests, heads),
        P(requests, heads, None, None),
        P(requests, heads, None),
        P(requests, heads, None),
        P(requests, heads, None),
        P(heads, "seq"),
        P(),
        tokens,
        tokens,
        owned,
        owned,
        owned,
    )
    return jax.shard_map(
        on_device, mesh=fine, in_specs=placed, out_specs=tokens, check_vma=False
    )
```

```python
import functools

import jax
import jax.numpy as jnp
from jax import lax
from jax.experimental import pallas as pl
from jax.experimental.pallas import tpu as pltpu
from jax.sharding import Mesh
from jax.sharding import PartitionSpec as P

epsilon = 1e-06
LANES = 128
OFFSET_NS = 13500
ATT_BLOCK = 32
ATT_PARTS = (3, 1)
MESH_AXES = ("zl", "core", "seq", "zh", "y")
PLANE = ("seq", "y")
HEADS = ("zl", "core")
STEPS = (0, 1, 3, 2)


def grant(mib):
    return pltpu.CompilerParams(vmem_limit_bytes=mib * 2**20)


def in_hbm(*arrays):
    return [pltpu.with_memory_space_constraint(a, pltpu.HBM) for a in arrays]


def iota(shape, dim):
    return lax.broadcasted_iota(jnp.int32, shape, dim)


def div(a, b):
    return lax.div(a, jnp.full_like(a, b))


def rem(a, b):
    return lax.rem(a, jnp.full_like(a, b))


def attention_body(slots_ref, counts_ref, query_ref, cache_ref, fresh_ref, out_ref, bias_ref, *, first):
    rows, _, positions, pair = cache_ref.shape
    head_dim = pair // 2
    group = query_ref.shape[1] // head_dim
    scale = head_dim ** (-0.5)
    step = pl.program_id(0)

    @pl.when(step == 0)
    def _():
        listed, all_rows = slots_ref.shape
        segments = counts_ref.shape[0]
        keep = listed // segments
        seg_length = positions // segments
        counts = counts_ref[...].astype(jnp.float32)
        limit = jnp.concatenate(
            [jnp.broadcast_to(counts[s : s + 1], (keep, all_rows)) for s in range(segments)], axis=0
        )
        rank = rem(iota((listed, all_rows), 0), keep).astype(jnp.float32)
        valid = jnp.where(rank < limit, slots_ref[...].astype(jnp.float32), 99.0)
        valid = valid.astype(jnp.bfloat16)
        place = rem(iota((positions, all_rows), 0), seg_length).astype(jnp.float32)
        source = iota((positions, listed), 1)
        wanted = div(iota((positions, listed), 0), seg_length) * keep
        bias = jnp.full((positions, all_rows), -1e30, jnp.float32)
        for j in range(keep):
            pick = jnp.where(source == wanted + j, 1.0, 0.0).astype(jnp.bfloat16)
            here = jnp.dot(pick, valid, preferred_element_type=jnp.float32)
            bias = jnp.where(here == place, 0.0, bias)
        bias_ref[...] = bias.T

    query = query_ref[...].reshape(rows, group, head_dim)
    keys = cache_ref[:, 0, :, :head_dim]
    values = cache_ref[:, 0, :, head_dim:]
    fresh = fresh_ref[...].astype(jnp.float32)
    both = jnp.einsum(
        "rgd,rpd->rgp",
        query.reshape(rows // 2, 2 * group, head_dim),
        keys.reshape(rows // 2, 2 * positions, head_dim),
        preferred_element_type=jnp.float32,
    )
    scores = jnp.stack([both[:, :group, :positions], both[:, group:, positions:]], axis=1)
    scores = scores.reshape(rows, group, positions) * scale
    bias = bias_ref[pl.ds(pl.multiple_of((first + step) * rows, rows), rows), :]
    scores = scores + bias[:, None, :]
    own = jnp.sum(
        query.astype(jnp.float32) * fresh[:, None, :head_dim], axis=-1, keepdims=True
    ) * scale
    top = jnp.maximum(jnp.max(scores, axis=-1, keepdims=True), own)
    probs = jnp.exp(scores - top).astype(jnp.bfloat16)
    take_new = jnp.exp(own - top)
    denom = jnp.sum(probs.astype(jnp.float32), axis=-1, keepdims=True) + take_new
    numer = jnp.einsum("rgp,rpd->rgd", probs, values, preferred_element_type=jnp.float32)
    numer = numer + take_new * fresh[:, None, head_dim:]
    out_ref[...] = (numer / denom).astype(jnp.bfloat16).reshape(rows, group * head_dim)


def attention(slots, counts, queries, cache_pairs, fresh, first, steps):
    rows, width = queries.shape
    block = ATT_BLOCK
    return pl.pallas_call(
        functools.partial(attention_body, first=first),
        grid=(steps,),
        in_specs=[
            pl.BlockSpec(slots.shape, lambda i: (0, 0)),
            pl.BlockSpec(counts.shape, lambda i: (0, 0)),
            pl.BlockSpec((block, width), lambda i: (first + i, 0)),
            pl.BlockSpec((block,) + cache_pairs.shape[1:], lambda i: (first + i, 0, 0, 0)),
            pl.BlockSpec((block, fresh.shape[1]), lambda i: (first + i, 0)),
        ],
        out_specs=pl.BlockSpec((block, width), lambda i: (i, 0)),
        out_shape=jax.ShapeDtypeStruct((steps * block, width), jnp.bfloat16),
        scratch_shapes=[pltpu.VMEM((rows, cache_pairs.shape[2]), jnp.float32)],
        compiler_params=grant(24),
        name="attention",
    )(*in_hbm(slots, counts, queries, cache_pairs, fresh))


def project_body(here_ref, *refs):
    *head_refs, weight_ref, out_ref = refs
    earlier_ref = None
    if len(head_refs) > len(STEPS):
        earlier_ref, *head_refs = head_refs
    count, half = len(STEPS), head_refs[0].shape[0]
    heads = jnp.concatenate([r[...] for r in head_refs], axis=0)
    made = jnp.dot(heads, weight_ref[...], preferred_element_type=jnp.float32)
    made = made.astype(jnp.bfloat16)
    start = 0
    if earlier_ref is not None:
        start = earlier_ref.shape[1]
        out_ref[:, :start] = earlier_ref[...]
    for n, step in enumerate(STEPS):
        at = (here_ref[0] + (count - step)) & (count - 1)
        out_ref[at, start : start + half] = made[n * half : (n + 1) * half]


def project(here, earlier, blocks, weight):
    rows = blocks[0].shape[0] + sum(e.shape[1] for e in earlier)
    operands = [*earlier, *blocks, weight]
    return pl.pallas_call(
        project_body,
        in_specs=[pl.BlockSpec(memory_space=pltpu.SMEM)]
        + [pl.BlockSpec(memory_space=pltpu.VMEM)] * len(operands),
        out_shape=jax.ShapeDtypeStruct((len(blocks), rows, weight.shape[1]), jnp.bfloat16),
        compiler_params=grant(12),
        name="project",
    )(here, *operands)


def norm_body(here_ref, parts_ref, stream_ref, gain_ref, routes_ref, codes_ref, residual_ref, payload_ref):
    seqs, heads, rows, width = parts_ref.shape
    wide = seqs * width
    total = jnp.zeros((rows, 1), jnp.float32)
    for s in range(seqs):
        at = slice(s * width, (s + 1) * width)
        attn = parts_ref[s, 0].astype(jnp.float32)
        for h in range(1, heads):
            attn = attn + parts_ref[s, h].astype(jnp.float32)
        residual = (stream_ref[:, at].astype(jnp.float32) + attn).astype(jnp.bfloat16)
        residual_ref[:, at] = residual
        widened = residual.astype(jnp.float32)
        total = total + jnp.sum(widened * widened, axis=-1, keepdims=True)
    factor = lax.rsqrt(total / wide + epsilon)
    for s in range(seqs):
        at = slice(s * width, (s + 1) * width)
        widened = residual_ref[:, at].astype(jnp.float32)
        normed = (widened * factor * gain_ref[:, at]).astype(jnp.bfloat16)
        payload_ref[:, at] = normed
    top = routes_ref.shape[0]
    tail = jnp.concatenate(
        [
            routes_ref[...].astype(jnp.float32),
            codes_ref[...].astype(jnp.float32),
            jnp.zeros((LANES - 2 * top, rows), jnp.float32),
        ],
        axis=0,
    )
    payload_ref[:, wide:] = tail.T.astype(jnp.bfloat16)

    @pl.when(here_ref[2] == 1)
    def _():
        pl.delay(OFFSET_NS)


def norm(here, parts, stream, gain, routes, codes):
    rows, wide = stream.shape
    return pl.pallas_call(
        norm_body,
        in_specs=[pl.BlockSpec(memory_space=pltpu.SMEM)]
        + [pl.BlockSpec(memory_space=pltpu.VMEM)] * 5,
        out_shape=[
            jax.ShapeDtypeStruct((rows, wide), jnp.bfloat16),
            jax.ShapeDtypeStruct((rows, wide + LANES), jnp.bfloat16),
        ],
        compiler_params=grant(8),
        name="norm",
    )(here, parts, stream, gain, routes, codes)


def placement(tail, zh, blocks, top, experts_shape, capacity):
    seqs, zs, ys = experts_shape
    tokens = tail.shape[0]
    rows = tokens // blocks
    experts = seqs * ys
    slots = experts * blocks * capacity
    column = iota((tokens, experts), 1)
    name = (div(column, ys) * zs + zh) * ys + rem(column, ys)
    name = name.astype(jnp.float32)
    match = jnp.zeros((tokens, experts), jnp.float32)
    code = jnp.zeros((tokens, experts), jnp.float32)
    for k in range(top):
        hit = tail[:, k : k + 1] == name
        match = jnp.where(hit, 1.0, match)
        code = jnp.where(hit, tail[:, top + k : top + k + 1], code)
    row, col = iota((tokens, tokens), 0), iota((tokens, tokens), 1)
    before = jnp.where((div(row, rows) == div(col, rows)) & (col < row), 1.0, 0.0)
    rank = jnp.dot(
        before.astype(jnp.bfloat16), match.astype(jnp.bfloat16), preferred_element_type=jnp.float32
    )
    rank = jnp.where(match > 0.0, rank, 99.0)
    spread = jnp.where(
        div(iota((experts, slots), 1), blocks * capacity) == iota((experts, slots), 0), 1.0, 0.0
    ).astype(jnp.bfloat16)
    rank = jnp.dot(rank.astype(jnp.bfloat16), spread, preferred_element_type=jnp.float32)
    code = jnp.dot(code.astype(jnp.bfloat16), spread, preferred_element_type=jnp.float32)
    slot = rem(iota((tokens, slots), 1), blocks * capacity)
    at = div(iota((tokens, slots), 0), rows) * capacity + rank.astype(jnp.int32)
    return jnp.where((slot == at) & (rank < capacity), code, 0.0)


def dispatch_body(here_ref, *refs, static):
    *payload_refs, out_ref, code_ref, total_ref = refs
    planes = len(payload_refs)
    wide = out_ref.shape[1]
    top = static["top"]
    tail = jnp.concatenate([r[:, wide:].astype(jnp.float32) for r in payload_refs], axis=0)
    code = placement(tail, here_ref[1], planes, **static)
    place = jnp.where(code > 0.0, 1.0, 0.0).astype(jnp.bfloat16)
    tokens = jnp.concatenate([r[:, :wide] for r in payload_refs], axis=0)
    sent = lax.dot_general(
        place, tokens, (((0,), (0,)), ((), ())), preferred_element_type=jnp.float32
    )
    out_ref[...] = sent.astype(jnp.bfloat16)
    code_ref[...] = code.astype(jnp.bfloat16)
    lane = iota(tail.shape, 1)
    listed = jnp.where((lane >= top) & (lane < 2 * top), tail, 0.0)
    total_ref[...] = jnp.broadcast_to(jnp.sum(listed, axis=-1, keepdims=True), tail.shape)


def dispatch(here, payloads, static):
    seqs, _, ys = static["experts_shape"]
    planes, rows, wide = len(payloads), payloads[0].shape[0], payloads[0].shape[1] - LANES
    tokens, slots = planes * rows, seqs * ys * planes * static["capacity"]
    out, code, total = pl.pallas_call(
        lambda *refs: dispatch_body(*refs, static=static),
        in_specs=[pl.BlockSpec(memory_space=pltpu.SMEM)]
        + [pl.BlockSpec(memory_space=pltpu.VMEM)] * planes,
        out_shape=[
            jax.ShapeDtypeStruct((slots, wide), jnp.bfloat16),
            jax.ShapeDtypeStruct((tokens, slots), jnp.bfloat16),
            jax.ShapeDtypeStruct((tokens, LANES), jnp.float32),
        ],
        compiler_params=grant(16),
        name="dispatch",
    )(here, *payloads)
    return out.reshape(seqs * ys, -1, wide), (code, total)


def expert_body(rows_ref, gate_ref, up_ref, down_hbm, out_ref, down_ref, sem):
    fetch = pltpu.make_async_copy(down_hbm.at[0], down_ref, sem)
    fetch.start()
    rows = rows_ref[...]
    gate = jnp.dot(rows, gate_ref[0], preferred_element_type=jnp.float32)
    up = jnp.dot(rows, up_ref[0], preferred_element_type=jnp.float32)
    act = (gate / (1.0 + jnp.exp(-gate)) * up).astype(jnp.bfloat16)
    fetch.wait()
    part = jnp.dot(act, down_ref[...], preferred_element_type=jnp.float32)
    out_ref[...] = part.astype(jnp.bfloat16)


def expert(arrived, gate_weight, up_weight, down_weight):
    shape = arrived.shape
    wide = shape[-1]
    rows = shape[0] * shape[1]
    return pl.pallas_call(
        expert_body,
        in_specs=[pl.BlockSpec(memory_space=pltpu.VMEM)] * 3 + [pl.BlockSpec(memory_space=pl.ANY)],
        out_shape=jax.ShapeDtypeStruct((rows, wide), jnp.bfloat16),
        scratch_shapes=[
            pltpu.VMEM(down_weight.shape[1:], jnp.bfloat16),
            pltpu.SemaphoreType.DMA,
        ],
        compiler_params=grant(24),
        name="expert",
    )(
        arrived.reshape(rows, wide),
        pltpu.with_memory_space_constraint(gate_weight, pltpu.VMEM),
        pltpu.with_memory_space_constraint(up_weight, pltpu.VMEM),
        *in_hbm(down_weight),
    ).reshape(shape)


def combine_body(code_ref, total_ref, returned_ref, *outs):
    part = jnp.dot(code_ref[...], returned_ref[...], preferred_element_type=jnp.float32)
    part = (part / total_ref[:, :1]).astype(jnp.bfloat16)
    rows = part.shape[0] // len(outs)
    for b, out_ref in enumerate(outs):
        out_ref[...] = part[b * rows : (b + 1) * rows]


def combine(code, total, returned, planes):
    wide = returned.shape[-1]
    rows = code.shape[0] // planes
    return pl.pallas_call(
        combine_body,
        out_shape=[jax.ShapeDtypeStruct((rows, wide), jnp.bfloat16)] * planes,
        compiler_params=grant(10),
        name="combine",
    )(code, total, returned.reshape(-1, wide))


def finish_body(residual_ref, *refs):
    *sum_refs, out_ref = refs
    part = residual_ref[...].astype(jnp.float32)
    for ref in sum_refs:
        part = part + ref[...].astype(jnp.float32)
    out_ref[...] = part.astype(jnp.bfloat16)


def finish(residual, *sums):
    return pl.pallas_call(
        finish_body,
        out_shape=jax.ShapeDtypeStruct(residual.shape, jnp.bfloat16),
        compiler_params=grant(8),
        name="finish",
    )(residual, *sums)


def shift(size, by):
    return [(i, (i + by) % size) for i in range(size)]


def z_moves(lows, highs):
    size = lows * highs

    def index(z):
        return z % size % lows * highs + z % size // lows

    return [
        [(index(z), index(z + (far if z % lows == 0 else -far))) for z in range(size)]
        for far in (2, -1, -3)
    ]


def exchange(blocks, axes):
    return lax.all_to_all(blocks, axes, split_axis=0, concat_axis=0, tiled=True)


def on_device(
    stream,
    queries,
    cache_pairs,
    fresh_pairs,
    kept_slots,
    segment_kept_count,
    output_weight,
    norm_gain,
    routes,
    gate_codes,
    gate_weight,
    up_weight,
    down_weight,
):
    rows, wide = stream.shape
    seqs, zs, ys = (lax.axis_size(a) for a in ("seq", "zh", "y"))
    here = jnp.stack([lax.axis_index(a) for a in ("seq", "zh", "core")]).astype(jnp.int32)
    experts = seqs * zs * ys
    static = dict(
        top=routes.shape[1],
        experts_shape=(seqs, zs, ys),
        capacity=min(rows, max(2, 2 * rows * routes.shape[1] // experts)),
    )

    made = []
    for part, steps in enumerate(ATT_PARTS):
        head_out = attention(
            kept_slots[:, 0].T,
            segment_kept_count[:, 0].T,
            queries,
            cache_pairs,
            fresh_pairs[:, 0],
            sum(ATT_PARTS[:part]),
            steps,
        )
        blocks = [head_out] + [lax.ppermute(head_out, "seq", shift(seqs, d)) for d in STEPS[1:]]
        made = [project(here, made, blocks, output_weight)]
    parts = made[0]
    parts = exchange(parts.reshape(-1, rows, parts.shape[-1]), ("seq",) + HEADS)
    parts = parts.reshape(seqs, -1, rows, parts.shape[-1])
    residual, payload = norm(
        here, parts, stream, norm_gain.reshape(1, -1), routes.T, gate_codes.T
    )
    moves = z_moves(lax.axis_size("zl"), zs)
    payloads = [payload] + [lax.ppermute(payload, ("zl", "zh"), m) for m in moves]
    sent, mix = dispatch(here, payloads, static)
    made = expert(exchange(sent, PLANE), gate_weight, up_weight, down_weight)
    own, *sums = combine(*mix, exchange(made, PLANE), len(payloads))
    back = [[(b, a) for a, b in m] for m in moves]
    sums = [lax.ppermute(v, ("zl", "zh"), m) for v, m in zip(sums, back)]
    return finish(residual, own, *sums)


def solution(mesh):
    fine = Mesh(mesh.devices.reshape(2, 2, mesh.shape["seq"], 4, 4), MESH_AXES)
    heads, req = HEADS, ("zh", "y")
    tokens = P(req + ("seq",) + heads, None)
    requests = req + ("seq",)
    owned = P(("seq",) + req, None, None)
    placed = (
        tokens,
        P(requests, heads),
        P(requests, heads, None, None),
        P(requests, heads, None),
        P(requests, heads, None),
        P(requests, heads, None),
        P(heads, "seq"),
        P(),
        tokens,
        tokens,
        owned,
        owned,
        owned,
    )
    return jax.shard_map(
        on_device, mesh=fine, in_specs=placed, out_specs=tokens, check_vma=False
    )
```
